1024 devices in a mesh: seq: 128 (over z, x, core), head: 8 (over y).
Axes of the slice: x: 4, y: 8, z: 16, core: 2. Of those that a mesh axis runs over, the one named last changes fastest.
Arguments:
- grad_out: bfloat16 [16384, 3072], P('seq', 'head'), may hold values from -6 to 6
- out_weight: bfloat16 [3072, 3072], P('head', 'seq'), may hold values from -0.109375 to 0.109375
- row_owner: int32 [16384], P('seq'), may hold values from 0 to 127, as said below
- row_position: int32 [16384], P('seq'), may hold values from 0 to 127, as said below
- query_rows: bfloat16 [16384, 3072], P('seq', 'head'), may hold values from -48 to 48
- key_rows: bfloat16 [16384, 3072], P('seq', 'head'), may hold values from -48 to 48
- value_rows: bfloat16 [16384, 3072], P('seq', 'head'), may hold values from -6 to 6
- band_widths: int32 [128, 2], P('seq'), may hold values from 16 to 64, as said below
Outputs:
- grad_query: bfloat16 [16384, 3072], P('seq', 'head')
- grad_key: bfloat16 [16384, 3072], P('seq', 'head')
- grad_value: bfloat16 [16384, 3072], P('seq', 'head')
The draws below stay inside these ranges and needn't reach their ends.
Inputs may be any that keep to these rules, and one draw needn't show every extreme that they name: `row_owner`: each frame receives each of its 128 positions from exactly one packed row. One device holds at most 1 row of one frame, and every device holds exactly 1 row of some frame; how many rows device s holds of frame o depends only on (o - s) mod 128, and is at least one for (o - s) mod 128 equal to 1, 64 and 127. `row_position`: together with row_owner, a permutation of all tokens. `band_widths`: column 0 lies in 32 to 64, column 1 in 16 to 32.
All inputs are finite; a program needn't handle non-finite values.
Results may differ from the reference program's by a relative error of at most 0.0088.
Values may be sent and summed in bfloat16 or wider, within the bound.
No kernel may reach another device: no remote copies, remote signals or barrier semaphores. Data moves between devices by JAX's collectives and lax.ppermute only.
A program may use at most 32 MiB of HBM per device.

```python
import jax
import jax.numpy as jnp
from jax import lax

D = 3072
HEADS = 24
HEAD_DIM = 128
FRAME_TOK = 128
FRAMES = 128
TOKENS = 16384
CAP = 1


def routing(key):
    folded = jax.random.fold_in(key, 11)
    key_vals, key_pick, key_slots, key_places = jax.random.split(folded, 4)
    ranking = jax.random.permutation(key_vals, FRAMES)
    ranking = ranking.at[FRAMES // 2].set(-3)
    ranking = ranking.at[1].set(-2)
    ranking = ranking.at[FRAMES - 1].set(-1)
    order_vals = jnp.argsort(ranking, stable=True)
    offsets_all = jnp.repeat(order_vals, CAP)
    remaining = jax.random.permutation(key_pick, FRAMES * CAP - 3 * CAP) + 3 * CAP
    chosen = jnp.concatenate([jnp.arange(CAP), jnp.array([CAP, 2 * CAP]), remaining[:FRAME_TOK - CAP - 2]])
    offsets = offsets_all[chosen]

    def shuffled(subkey):
        return jax.random.permutation(subkey, FRAME_TOK)
    slot_order = jax.vmap(shuffled)(jax.random.split(key_slots, FRAMES))
    places = jax.vmap(shuffled)(jax.random.split(key_places, FRAMES))
    device = jnp.arange(FRAMES)[:, None]
    owner = (device + offsets[slot_order]) % FRAMES
    position = places[owner, slot_order]
    return (owner.reshape(-1).astype(jnp.int32), position.reshape(-1).astype(jnp.int32))


def draw_row_owner(key, part):
    return routing(key)[0]


def draw_row_position(key, part):
    return routing(key)[1]


def draw_band_widths(key, part):
    folded = jax.random.fold_in(key, 23)
    key_half, key_quarter, key_frame = jax.random.split(folded, 3)
    half = jax.random.randint(key_half, (FRAMES,), FRAME_TOK // 4, FRAME_TOK // 2 + 1)
    quarter = jax.random.randint(key_quarter, (FRAMES,), FRAME_TOK // 8, FRAME_TOK // 4 + 1)
    chosen = jax.random.randint(key_frame, (), 0, FRAMES)
    marked = jnp.arange(FRAMES) == chosen
    half = jnp.where(marked, FRAME_TOK // 2, half)
    quarter = jnp.where(marked, FRAME_TOK // 8, quarter)
    return jnp.stack([half, quarter], axis=1).astype(jnp.int32)


def attention_pair(key):
    folded = jax.random.fold_in(key, 31)
    subkeys = jax.random.split(folded, 2)
    layout = (TOKENS, HEADS, HEAD_DIM)
    queries = jnp.clip(jax.random.normal(subkeys[0], layout, jnp.float32), -6.0, 6.0)
    keys_all = jnp.clip(jax.random.normal(subkeys[1], layout, jnp.float32), -6.0, 6.0)
    return (queries.reshape(TOKENS, D), keys_all.reshape(TOKENS, D))


def draw_query_rows(key, part):
    return attention_pair(key)[0].astype(jnp.bfloat16)


def draw_key_rows(key, part):
    return attention_pair(key)[1].astype(jnp.bfloat16)


def levels(own_key, shape, cuts, low, largest):
    gain = 1.0
    for dim, parts in cuts:
        steps = jax.random.uniform(jax.random.fold_in(jax.random.fold_in(own_key, 6), dim), (parts,), jnp.float32, low / len(cuts), largest / len(cuts))
        gain = gain * jnp.repeat(jnp.exp(steps), shape[dim] // parts).reshape((-1,) + (1,) * (len(shape) - 1 - dim))
    return gain


def centred(stream_key, shape, width, most, cuts=(), kind=jnp.bfloat16):
    result = jax.random.normal(stream_key, shape, jnp.float32) * width
    if len(cuts) > 0:
        result = levels(stream_key, shape, cuts, -0.22, 0.18) * result
    return jnp.clip(result, min=-most, max=most).astype(kind)


def setup_inputs(seed: int = 0) -> dict:
    key_list = jax.random.split(jax.random.key(seed), 9)
    return {
        "grad_out": centred(key_list[0], (TOKENS, D), 1.0, 6.0, ((0, 128), (1, 8))),
        "out_weight": centred(key_list[1], (D, D), D ** -0.5, 0.109375, ((0, 8), (1, 128))),
        "row_owner": draw_row_owner(jax.random.fold_in(key_list[8], 71), 0),
        "row_position": draw_row_position(jax.random.fold_in(key_list[8], 71), 0),
        "query_rows": draw_query_rows(jax.random.fold_in(key_list[8], 71), 0),
        "key_rows": draw_key_rows(jax.random.fold_in(key_list[8], 71), 0),
        "value_rows": centred(key_list[6], (TOKENS, D), 1.0, 6.0, ((0, 128), (1, 8))),
        "band_widths": draw_band_widths(jax.random.fold_in(key_list[8], 71), 0),
    }


DISTANCES = (0, 1, 2, 4)
NEG_FILL = -1.0e30


def reference(grad_out, out_weight, row_owner, row_position, query_rows, key_rows, value_rows, band_widths):
    packed = jnp.dot(grad_out, out_weight.T, preferred_element_type=jnp.float32).astype(jnp.bfloat16)
    target = (row_owner * FRAME_TOK + row_position).astype(jnp.int32)
    grad_attn = jnp.zeros_like(packed).at[target].set(packed)
    scale = HEAD_DIM ** -0.5
    margin = 4 * FRAME_TOK

    def padded(array):
        return jnp.pad(array, ((margin, margin), (0, 0)))

    query_pad = padded(query_rows)
    key_pad = padded(key_rows)
    value_pad = padded(value_rows)
    grad_pad = padded(grad_attn)
    positions = jnp.arange(FRAME_TOK, dtype=jnp.int32)
    spread = jnp.abs(positions[:, None] - positions[None, :])

    def frame_rows(array, frame):
        start = ((frame + 4) * FRAME_TOK).astype(jnp.int32)
        return lax.dynamic_slice_in_dim(array, start, FRAME_TOK, 0)

    def split_heads(array):
        return array.astype(jnp.float32).reshape(FRAME_TOK, HEADS, HEAD_DIM)

    def allowed(frame, distance):
        in_range = (frame - distance >= 0) & (frame < FRAMES)
        clipped = jnp.clip(frame, 0, FRAMES - 1)
        if distance == 2:
            limit = band_widths[clipped, 0]
        elif distance == 4:
            limit = band_widths[clipped, 1]
        else:
            limit = FRAME_TOK
        return (in_range & (spread < limit))[None]

    def logits(query_frame, key_frame):
        return jnp.einsum("ihc,jhc->hij", split_heads(query_frame), split_heads(key_frame)) * scale

    def to_half(array):
        return lax.optimization_barrier(array.astype(jnp.bfloat16)).astype(jnp.float32)

    def statistics(frame):
        queries = frame_rows(query_pad, frame)
        score_list = []
        mask_list = []
        value_list = []
        for distance in DISTANCES:
            score_list.append(logits(queries, frame_rows(key_pad, frame - distance)))
            mask_list.append(allowed(frame, distance))
            value_list.append(split_heads(frame_rows(value_pad, frame - distance)))
        scores = jnp.concatenate(score_list, axis=2)
        usable = jnp.concatenate(mask_list, axis=2)
        row_max = jnp.max(jnp.where(usable, scores, NEG_FILL), axis=2, keepdims=True)
        weights = jnp.where(usable, jnp.exp(scores - row_max), 0.0)
        row_sum = jnp.sum(weights, axis=2, keepdims=True)
        prob_half = to_half(weights / row_sum)
        values_all = jnp.concatenate(value_list, axis=0)
        attn_out = jnp.einsum("hij,jhc->ihc", prob_half, values_all)
        row_dot = jnp.sum(split_heads(frame_rows(grad_pad, frame)) * attn_out, axis=2).T
        return (row_max + jnp.log(row_sum))[:, :, 0], row_dot

    frames = jnp.arange(FRAMES, dtype=jnp.int32)
    log_norm, row_dots = lax.map(statistics, frames)

    def grad_queries(frame):
        queries = frame_rows(query_pad, frame)
        grads = split_heads(frame_rows(grad_pad, frame))
        norm_here = log_norm[frame][:, :, None]
        dot_here = row_dots[frame][:, :, None]
        total = jnp.zeros((FRAME_TOK, HEADS, HEAD_DIM), jnp.float32)
        for distance in DISTANCES:
            keys = frame_rows(key_pad, frame - distance)
            values = frame_rows(value_pad, frame - distance)
            prob = jnp.where(allowed(frame, distance), jnp.exp(logits(queries, keys) - norm_here), 0.0)
            grad_prob = jnp.einsum("ihc,jhc->hij", grads, split_heads(values))
            grad_score = to_half(prob * (grad_prob - dot_here))
            total = total + jnp.einsum("hij,jhc->ihc", grad_score, split_heads(keys))
        return (scale * total).reshape(FRAME_TOK, D).astype(jnp.bfloat16)

    def grad_keys(frame):
        keys = frame_rows(key_pad, frame)
        values = frame_rows(value_pad, frame)
        key_total = jnp.zeros((FRAME_TOK, HEADS, HEAD_DIM), jnp.float32)
        value_total = jnp.zeros((FRAME_TOK, HEADS, HEAD_DIM), jnp.float32)
        for distance in DISTANCES:
            source = frame + distance
            queries = frame_rows(query_pad, source)
            grads = split_heads(frame_rows(grad_pad, source))
            clipped = jnp.clip(source, 0, FRAMES - 1)
            norm_here = log_norm[clipped][:, :, None]
            dot_here = row_dots[clipped][:, :, None]
            prob = jnp.where(allowed(source, distance), jnp.exp(logits(queries, keys) - norm_here), 0.0)
            value_total = value_total + jnp.einsum("hij,ihc->jhc", to_half(prob), grads)
            grad_prob = jnp.einsum("ihc,jhc->hij", grads, split_heads(values))
            grad_score = to_half(prob * (grad_prob - dot_here))
            key_total = key_total + jnp.einsum("hij,ihc->jhc", grad_score, split_heads(queries))
        return ((scale * key_total).reshape(FRAME_TOK, D).astype(jnp.bfloat16),
                value_total.reshape(FRAME_TOK, D).astype(jnp.bfloat16))

    grad_query = lax.map(grad_queries, frames).reshape(TOKENS, D)
    key_part, value_part = lax.map(grad_keys, frames)
    return grad_query, key_part.reshape(TOKENS, D), value_part.reshape(TOKENS, D)
```

```python
import jax
import jax.numpy as jnp
from jax import lax
from jax.sharding import Mesh
from jax.sharding import PartitionSpec as P

HEAD_DIM = 128


DISTANCES = (0, 1, 2, 4)
NEG_FILL = -1e30
SEQ = ("z", "x", "core")
F32 = jnp.float32
BF16 = jnp.bfloat16


def shifted(value, by):
    peers = lax.axis_size(SEQ)
    pairs = [(i, i + by) for i in range(peers) if 0 <= i + by < peers]
    return lax.ppermute(value, SEQ, pairs)


def exchange(value, axis):
    return lax.all_to_all(value, axis, split_axis=0, concat_axis=0, tiled=True)


def spread_to(value, axis):
    peers = lax.axis_size(axis)
    return exchange(jnp.broadcast_to(value[None], (peers,) + value.shape), axis)


def three_parts(value):
    high = lax.reduce_precision(value, 8, 7)
    rest = value - high
    middle = lax.reduce_precision(rest, 8, 7)
    return [high.astype(BF16), middle.astype(BF16), (rest - middle).astype(BF16)]


def dot(a, b, dims):
    return lax.dot_general(a, b, (dims, ((), ())), preferred_element_type=F32)


def per_device(
    grad_out, out_weight, row_owner, row_position, query_rows, key_rows, value_rows, band_widths
):
    frame_len = query_rows.shape[0]
    width = query_rows.shape[1]
    heads = width // HEAD_DIM
    scale = HEAD_DIM ** (-0.5)
    frames = lax.axis_size(SEQ)
    frame = lax.axis_index(SEQ)

    w_block = out_weight.T
    w_z = spread_to(w_block, "z")
    w_zx = spread_to(w_z, "x")
    w_all = spread_to(w_zx, "core")
    weight = jnp.transpose(w_all, (2, 1, 0, 3, 4)).reshape(-1, width)

    sel = (row_owner[None, :] == jnp.arange(frames)[:, None]).astype(BF16)
    tagged = jnp.concatenate(
        [grad_out, jnp.broadcast_to(row_position[:, None].astype(BF16), (frame_len, 128))], axis=1
    )
    outgoing = dot(sel, tagged, ((1,), (0,))).astype(BF16)
    incoming = exchange(outgoing.reshape(frames, 1, width + 128), SEQ).reshape(frames, width + 128)
    places = incoming[:, width].astype(F32)
    land = (places[None, :] == jnp.arange(frame_len, dtype=F32)[:, None]).astype(BF16)
    rows = dot(land, incoming[:, :width], ((1,), (0,))).astype(BF16)
    rows_all = spread_to(rows, "head")

    pair = jnp.concatenate([key_rows, value_rows], axis=1)
    pairs_all = [pair] + [shifted(pair, d) for d in DISTANCES[1:]]
    later_queries = [shifted(query_rows, -d) for d in DISTANCES[1:]]

    positions = jnp.arange(frame_len)
    spread = jnp.abs(positions[:, None] - positions[None, :])
    limits = {0: frame_len, 1: frame_len, 2: band_widths[0, 0], 4: band_widths[0, 1]}
    usable = jnp.concatenate(
        [(frame - d >= 0) & (spread < limits[d]) for d in DISTANCES], axis=1
    )

    def head_of(array, h):
        return array[:, h * HEAD_DIM : (h + 1) * HEAD_DIM]

    keys = jnp.concatenate([p[:, :width] for p in pairs_all], axis=0)
    values = jnp.concatenate([p[:, width:] for p in pairs_all], axis=0)
    probs, outs, norms = [], [], []
    for h in range(heads):
        scores = dot(head_of(query_rows, h), head_of(keys, h), ((1,), (1,))) * scale
        row_max = jnp.max(jnp.where(usable, scores, NEG_FILL), axis=1, keepdims=True)
        weights = jnp.where(usable, jnp.exp(scores - row_max), 0.0)
        row_sum = jnp.sum(weights, axis=1, keepdims=True)
        prob = weights / row_sum
        probs.append(prob)
        outs.append(dot(prob.astype(BF16), head_of(values, h), ((1,), (0,))))
        norms.append(row_max + jnp.log(row_sum))
    later_scores = [
        [dot(head_of(q, h), head_of(key_rows, h), ((1,), (1,))) * scale for h in range(heads)]
        for q in later_queries
    ]

    weight = weight.reshape(rows_all.shape[0], width, width)
    grad_attn = lax.dot_general(
        rows_all, weight, (((0, 2), (0, 1)), ((), ())), preferred_element_type=F32
    ).astype(BF16)

    dots = [
        jnp.sum(head_of(grad_attn, h).astype(F32) * outs[h], axis=1, keepdims=True)
        for h in range(heads)
    ]
    tail = three_parts(jnp.concatenate(norms, axis=1)) + three_parts(jnp.concatenate(dots, axis=1))
    tail.append(jnp.broadcast_to(band_widths.astype(BF16), (frame_len, 2)))
    tail.append(jnp.zeros((frame_len, 128 - 6 * heads - 2), BF16))
    parcel = jnp.concatenate([grad_attn] + tail, axis=1)
    later = [shifted(parcel, -d) for d in DISTANCES[1:]]

    grad_query, grad_key, grad_value = [], [], []
    for h in range(heads):
        own_grad = head_of(grad_attn, h)
        grad_prob = dot(own_grad, head_of(values, h), ((1,), (1,)))
        grad_score = (probs[h] * (grad_prob - dots[h])).astype(BF16)
        grad_query.append(scale * dot(grad_score, head_of(keys, h), ((1,), (0,))))
        key_sum = dot(grad_score[:, :frame_len], head_of(query_rows, h), ((0,), (0,)))
        value_sum = dot(probs[h][:, :frame_len].astype(BF16), own_grad, ((0,), (0,)))
        for slot, distance in enumerate(DISTANCES[1:]):
            box = later[slot]
            extra = box[:, width:].astype(F32)
            norm = extra[:, h : h + 1] + extra[:, heads + h : heads + h + 1]
            norm = norm + extra[:, 2 * heads + h : 2 * heads + h + 1]
            first = 3 * heads + h
            row_dot = extra[:, first : first + 1] + extra[:, first + heads : first + heads + 1]
            row_dot = row_dot + extra[:, first + 2 * heads : first + 2 * heads + 1]
            allowed = jnp.broadcast_to(frame + distance < frames, (frame_len, frame_len))
            if distance > 1:
                column = 6 * heads + (0 if distance == 2 else 1)
                allowed = allowed & (spread.astype(F32) < extra[:, column : column + 1])
            prob = jnp.where(
                allowed, jnp.exp(jnp.where(allowed, later_scores[slot][h] - norm, 0.0)), 0.0
            )
            box_grad = head_of(box, h)
            box_prob = dot(box_grad, head_of(value_rows, h), ((1,), (1,)))
            box_score = (prob * (box_prob - row_dot)).astype(BF16)
            key_sum = key_sum + dot(box_score, head_of(later_queries[slot], h), ((0,), (0,)))
            value_sum = value_sum + dot(prob.astype(BF16), box_grad, ((0,), (0,)))
        grad_key.append(scale * key_sum)
        grad_value.append(value_sum)
    return tuple(
        jnp.concatenate(parts, axis=1).astype(BF16) for parts in (grad_query, grad_key, grad_value)
    )


def solution(mesh):
    sizes = {"z": 16, "x": 4, "core": 2}
    grid = mesh.devices.reshape(tuple(sizes.values()) + (mesh.shape["head"],))
    fine = Mesh(grid, tuple(sizes) + ("head",))
    return jax.shard_map(
        per_device,
        mesh=fine,
        in_specs=(
            P(SEQ, "head"),
            P("head", SEQ),
            P(SEQ),
            P(SEQ),
            P(SEQ, "head"),
            P(SEQ, "head"),
            P(SEQ, "head"),
            P(SEQ, None),
        ),
        out_specs=(P(SEQ, "head"), P(SEQ, "head"), P(SEQ, "head")),
        check_vma=False,
    )
```

```python
import functools

import jax
import jax.numpy as jnp
from jax import lax
from jax.experimental import pallas as pl
from jax.experimental.pallas import tpu as pltpu
from jax.sharding import Mesh
from jax.sharding import PartitionSpec as P


HEAD_DIM = 128
LANES = 128
DISTANCES = (0, 1, 2, 4)
NEG_FILL = -1e30
SEQ = ("z", "x", "core")
SIZES = {"z": 16, "x": 4, "core": 2}
F32 = jnp.float32
BF16 = jnp.bfloat16
SCALE = HEAD_DIM ** (-0.5)


def shifted(value, by):
    peers = lax.axis_size(SEQ)
    pairs = [(i, i + by) for i in range(peers) if 0 <= i + by < peers]
    return lax.ppermute(value, SEQ, pairs)


def turned(value, axis, by):
    peers = lax.axis_size(axis)
    return lax.ppermute(value, axis, [(i, (i + by) % peers) for i in range(peers)])


def exchange(value, axis):
    return lax.all_to_all(value, axis, split_axis=0, concat_axis=0, tiled=True)


def dot(a, b, left, right):
    return lax.dot_general(a, b, (((left,), (right,)), ((), ())), preferred_element_type=F32)


def call(body, outs, spaces, args, flops):
    smem = pl.BlockSpec(memory_space=pltpu.SMEM)
    vmem = pl.BlockSpec(memory_space=pltpu.VMEM)
    size = sum(a.size * a.dtype.itemsize for a in args)
    size += sum(int(jnp.dtype(t).itemsize) * functools.reduce(lambda m, n: m * n, s) for s, t in outs)
    return pl.pallas_call(
        body,
        out_shape=[jax.ShapeDtypeStruct(s, t) for s, t in outs],
        in_specs=[smem if c == "s" else vmem for c in spaces],
        out_specs=[vmem] * len(outs),
        cost_estimate=pl.CostEstimate(flops=flops, bytes_accessed=size, transcendentals=0),
        compiler_params=pltpu.CompilerParams(vmem_limit_bytes=8 * 2**20),
    )(*args)


def iota(shape, dim):
    return lax.broadcasted_iota(jnp.int32, shape, dim)


def lanes(h):
    return slice(h * LANES, (h + 1) * LANES)


def pack_body(owner, position, grad, weight, key, value, out, pair):
    pick = iota((128, 128), 0) == owner[...]
    place = jnp.sum(jnp.where(pick, position[...].astype(F32), 0.0), axis=1, keepdims=True)
    place = jnp.broadcast_to(place, (128, LANES)).astype(BF16)
    rows = dot(pick.astype(BF16), grad[...], 1, 0).astype(BF16)
    for h in range(3):
        piece = weight[:, lanes(h)]
        for z in range(16):
            out[z, 24 * h : 24 * h + 24, :] = piece
            out[z, 72 + 8 * h : 80 + 8 * h, :] = rows[8 * z : 8 * z + 8, lanes(h)]
    for z in range(16):
        out[z, 96:104, :] = place[8 * z : 8 * z + 8]
    pair[:, :384] = key[...]
    pair[:, 384:] = value[...]


def split_body(got, weight, rows):
    weight[...] = got[:, :72, :]
    row, col = iota((128, 128), 0), iota((128, 128), 1)
    order = (col == (row & 15) * 8 + (row >> 4)).astype(BF16)
    for b in range(4):
        block = got[:, 72 + 8 * b : 80 + 8 * b, :].reshape(128, LANES)
        rows[:, :, lanes(b)] = dot(order, block, 1, 0).astype(BF16).reshape(8, 16, LANES)


def land_body(got, out):
    flat = got[...].reshape(128, 512)
    where = (flat[:, 384:].astype(F32) == iota((128, 128), 1).astype(F32)).astype(BF16)
    rows = dot(where, flat[:, :384], 0, 0).astype(BF16)
    for y in range(8):
        out[y] = rows


def forward_body(frame, band, query, key, value, b1, b2, b4, l1, l2, l4, prob, norm, score):
    spread = jnp.abs(iota((128, 128), 0) - iota((128, 128), 1))
    f = frame[0]
    limits = [
        None,
        jnp.where(f >= 1, 128, 0),
        jnp.where(f >= 2, band[0, 0], 0),
        jnp.where(f >= 4, band[0, 1], 0),
    ]
    for h in range(3):
        q = query[:, lanes(h)]
        parts = []
        for keys, limit in zip((key, b1, b2, b4), limits):
            s = dot(keys[:, lanes(h)], q, 1, 1) * SCALE
            parts.append(s if limit is None else jnp.where(spread < limit, s, NEG_FILL))
        s = jnp.concatenate(parts, axis=0)
        top = jnp.max(s, axis=0, keepdims=True)
        w = jnp.exp(s - top)
        total = jnp.sum(w, axis=0, keepdims=True)
        prob[h] = w / total
        norm[:, lanes(h)] = top + jnp.log(total)
        for i, later in enumerate((l1, l2, l4)):
            score[3 * i + h] = dot(key[:, lanes(h)], later[:, lanes(h)], 1, 1) * SCALE


def gather_body(frame, o0, o1, o2, o3, p0, p1, p2, p3, out):
    x, core = (frame[0] >> 1) & 3, frame[0] & 1
    for c, pieces in enumerate(((o0, o1, o2, o3), (p0, p1, p2, p3))):
        to_core = core if c == 0 else 1 - core
        for turn, piece in enumerate(pieces):
            to_x = (x + 4 - turn) & 3
            for h in range(3):
                out[:, to_x, to_core, :, lanes(h)] = piece[:, 24 * h : 24 * h + 24, :]


def parts_of(value):
    high = value.astype(BF16)
    rest = value - high.astype(F32)
    middle = rest.astype(BF16)
    return high, middle, (rest - middle.astype(F32)).astype(BF16)


def project_body(band, rows, weight, value, b1, b2, b4, prob, norm, parcel, row_dot):
    total = dot(rows[0], weight[0], 1, 0)
    for y in range(1, 8):
        total = total + dot(rows[y], weight[y], 1, 0)
    grad = total.astype(BF16)
    parcel[:128, :] = grad
    dots = []
    for h in range(3):
        g = grad[:, lanes(h)]
        whole = jnp.zeros((1, 128), F32)
        for i, values in enumerate((value, b1, b2, b4)):
            v = values[:, lanes(h)] if i == 0 else values[:, lanes(3 + h)]
            part = prob[h, 128 * i : 128 * i + 128].astype(BF16).astype(F32) * dot(v, g, 1, 1)
            whole = whole + jnp.sum(part, axis=0, keepdims=True)
        dots.append(whole)
    dots = jnp.concatenate(dots, axis=1)
    row_dot[...] = dots
    bands = [jnp.full((1, 384), band[0, i], jnp.int32).astype(F32) for i in range(2)]
    stack = [v.astype(F32) for v in parts_of(norm[...]) + parts_of(dots)] + bands
    parcel[128:, :] = jnp.concatenate(stack, axis=0).astype(BF16)


def own_body(parcel, row_dot, prob, query, key, value, b1, b2, b4, grad_query, key_part, value_part):
    for h in range(3):
        g = parcel[:128, lanes(h)]
        q = query[:, lanes(h)]
        total = None
        for i, pair in enumerate((None, b1, b2, b4)):
            k = key[:, lanes(h)] if i == 0 else pair[:, lanes(h)]
            v = value[:, lanes(h)] if i == 0 else pair[:, lanes(3 + h)]
            p = prob[h, 128 * i : 128 * i + 128]
            s = (p * (dot(v, g, 1, 1) - row_dot[:, lanes(h)])).astype(BF16)
            part = dot(s, k, 0, 0)
            total = part if total is None else total + part
            if i == 0:
                key_part[:, lanes(h)] = dot(s, q, 1, 0)
                value_part[:, lanes(h)] = dot(p.astype(BF16), g, 1, 0)
        grad_query[:, lanes(h)] = (SCALE * total).astype(BF16)


def later_body(frame, a1, a2, a4, l1, l2, l4, score, value, key_part, value_part, grad_key, grad_value):
    spread = jnp.abs(iota((128, 128), 0) - iota((128, 128), 1)).astype(F32)
    for h in range(3):
        keys, values = key_part[:, lanes(h)], value_part[:, lanes(h)]
        for i, (d, box, later) in enumerate(((1, a1, l1), (2, a2, l2), (4, a4, l4))):
            extra = box[128:, lanes(h)].astype(F32)
            norm = extra[0:1] + extra[1:2] + extra[2:3]
            row_dot = extra[3:4] + extra[4:5] + extra[5:6]
            limit = jnp.full((1, 128), 128.0, F32) if d == 1 else extra[5 + d // 2 : 6 + d // 2]
            limit = jnp.where(frame[0] + d < 128, limit, 0.0)
            p = jnp.where(spread < limit, jnp.exp(score[3 * i + h] - norm), 0.0)
            g = box[:128, lanes(h)]
            s = (p * (dot(value[:, lanes(h)], g, 1, 1) - row_dot)).astype(BF16)
            keys = keys + dot(s, later[:, lanes(h)], 1, 0)
            values = values + dot(p.astype(BF16), g, 1, 0)
        grad_key[:, lanes(h)] = (SCALE * keys).astype(BF16)
        grad_value[:, lanes(h)] = values.astype(BF16)


def step(
    grad_out, out_weight, row_owner, row_position, query_rows, key_rows, value_rows, band_widths
):
    frame = lax.axis_index(SEQ).reshape(1)

    packed, pair = call(
        pack_body,
        [((16, 104, LANES), BF16), ((128, 768), BF16)],
        "vvvvvv",
        (row_owner[None], row_position[None], grad_out, out_weight.T, key_rows, value_rows),
        13_000_000,
    )
    got = exchange(packed, "z")
    pairs, later = [], []
    for d in DISTANCES[1:]:
        pairs.append(shifted(pair, d))
    for d in DISTANCES[1:]:
        later.append(shifted(query_rows, -d))
    prob, norm, score = call(
        forward_body,
        [((3, 512, 128), F32), ((1, 384), F32), ((9, 128, 128), F32)],
        "ss" + "v" * 9,
        (frame, band_widths, query_rows, key_rows, value_rows, *pairs, *later),
        90_000_000,
    )
    got, prob, norm, score = lax.optimization_barrier((got, prob, norm, score))

    own, rows = call(split_body, [((16, 72, LANES), BF16), ((8, 16, 512), BF16)], "v", (got,), 17_000_000)
    rows = exchange(rows, ("x", "core"))
    (rows,) = call(land_body, [((8, 128, 384), BF16)], "v", (rows,), 13_000_000)
    rows = exchange(rows, "head")

    right = turned(own, "x", 1)
    left = turned(own, "x", -1)
    far = turned(right, "x", 1)
    pieces = [own, right, far, left]
    swapped = []
    for piece in pieces:
        swapped.append(turned(piece, "core", 1))
    (weight,) = call(gather_body, [((16, 4, 2, 24, 384), BF16)], "s" + "v" * 8, (frame, *pieces, *swapped), 0)
    rows, weight = lax.optimization_barrier((rows, weight))

    parcel, row_dot = call(
        project_body,
        [((136, 384), BF16), ((1, 384), F32)],
        "s" + "v" * 8,
        (band_widths, rows, weight.reshape(8, 384, 384), value_rows, *pairs, prob, norm),
        350_000_000,
    )
    boxes = []
    for d in DISTANCES[1:]:
        boxes.append(shifted(parcel, -d))
    grad_query, key_part, value_part = call(
        own_body,
        [((128, 384), BF16), ((128, 384), F32), ((128, 384), F32)],
        "v" * 9,
        (parcel, row_dot, prob, query_rows, key_rows, value_rows, *pairs),
        120_000_000,
    )
    grad_key, grad_value = call(
        later_body,
        [((128, 384), BF16), ((128, 384), BF16)],
        "s" + "v" * 10,
        (frame, *boxes, *later, score, value_rows, key_part, value_part),
        120_000_000,
    )
    return grad_query, grad_key, grad_value


def solution(mesh):
    grid = mesh.devices.reshape(tuple(SIZES.values()) + (mesh.shape["head"],))
    fine = Mesh(grid, tuple(SIZES) + ("head",))
    return jax.shard_map(
        step,
        mesh=fine,
        in_specs=(
            P(SEQ, "head"),
            P("head", SEQ),
            P(SEQ),
            P(SEQ),
            P(SEQ, "head"),
            P(SEQ, "head"),
            P(SEQ, "head"),
            P(SEQ, None),
        ),
        out_specs=(P(SEQ, "head"), P(SEQ, "head"), P(SEQ, "head")),
        check_vma=False,
    )
```

```python
import functools

import jax
import jax.numpy as jnp
from jax import lax
from jax.experimental import pallas as pl
from jax.experimental.pallas import tpu as pltpu
from jax.sharding import Mesh
from jax.sharding import PartitionSpec as P


HEAD_DIM = 128
LANES = 128
DISTANCES = (0, 1, 2, 4)
NEG_FILL = -1e30
SEQ = ("z", "x", "core")
SIZES = {"z": 16, "x": 4, "core": 2}
F32 = jnp.float32
BF16 = jnp.bfloat16
SCALE = HEAD_DIM ** (-0.5)


def shifted(value, by):
    peers = lax.axis_size(SEQ)
    pairs = [(i, i + by) for i in range(peers) if 0 <= i + by < peers]
    return lax.ppermute(value, SEQ, pairs)


def turned(value, axis, by):
    peers = lax.axis_size(axis)
    return lax.ppermute(value, axis, [(i, (i + by) % peers) for i in range(peers)])


def exchange(value, axis):
    return lax.all_to_all(value, axis, split_axis=0, concat_axis=0, tiled=True)


def dot(a, b, left, right):
    return lax.dot_general(a, b, (((left,), (right,)), ((), ())), preferred_element_type=F32)


SPACES = {"s": pltpu.SMEM, "v": pltpu.VMEM, "h": pltpu.HBM}


def call(body, outs, spaces, args, flops, scratch=(), copies=0):
    specs = [pl.BlockSpec(memory_space=SPACES[c]) for c in spaces]
    size = sum(a.size * a.dtype.itemsize for a in args)
    size += sum(int(jnp.dtype(t).itemsize) * functools.reduce(lambda m, n: m * n, s) for s, t in outs)
    args = [pltpu.with_memory_space_constraint(a, pltpu.HBM) if c == "h" else a for a, c in zip(args, spaces)]
    scratch = [pltpu.VMEM(shape, kind) for shape, kind in scratch]
    if copies:
        scratch.append(pltpu.SemaphoreType.DMA((copies,)))
    return pl.pallas_call(
        body,
        out_shape=[
            pltpu.HBM(s, t) if c == "h" else jax.ShapeDtypeStruct(s, t)
            for (s, t), c in zip(outs, spaces[len(args) :])
        ],
        in_specs=specs[: len(args)],
        out_specs=specs[len(args) :],
        scratch_shapes=scratch,
        cost_estimate=pl.CostEstimate(flops=flops, bytes_accessed=size, transcendentals=0),
        compiler_params=pltpu.CompilerParams(vmem_limit_bytes=8 * 2**20),
    )(*args)


def started(pairs, sems):
    copies = [pltpu.make_async_copy(a, b, sems.at[i]) for i, (a, b) in enumerate(pairs)]
    for copy in copies:
        copy.start()
    return copies


def wait(copies):
    for copy in copies:
        copy.wait()


def iota(shape, dim):
    return lax.broadcasted_iota(jnp.int32, shape, dim)


def lanes(h):
    return slice(h * LANES, (h + 1) * LANES)


def pack_body(frame, owner_h, place_h, grad_h, weight_h, key_h, value_h, out, pair, owner, place, grad, weight, sems):
    moves = ((owner_h, owner), (place_h, place), (grad_h, grad), (weight_h, weight))
    moves += ((key_h, pair.at[:, :384]), (value_h, pair.at[:, 384:]))
    copies = started(moves, sems)
    wait(copies[:4])
    pick = iota((128, 128), 0) == owner[...]
    where = jnp.sum(jnp.where(pick, place[...].astype(F32), 0.0), axis=1, keepdims=True)
    where = jnp.broadcast_to(where, (128, LANES)).astype(BF16)
    rows = dot(pick.astype(BF16), grad[...], 1, 0).astype(BF16)
    for h in range(3):
        piece = weight[:, lanes(h)]
        for z in range(16):
            out[z, 24 * h : 24 * h + 24, :] = piece
            out[z, 72 + 8 * h : 80 + 8 * h, :] = rows[8 * z : 8 * z + 8, lanes(h)]
    for z in range(16):
        out[z, 96:104, :] = where[8 * z : 8 * z + 8]
    wait(copies[4:])


def split_body(got, weight, rows, sems):
    copies = started(((got.at[:, :72, :], weight),), sems)
    row, col = iota((128, 128), 0), iota((128, 128), 1)
    order = (col == (row & 15) * 8 + (row >> 4)).astype(BF16)
    blocks = [
        dot(order, got[:, 72 + 8 * b : 80 + 8 * b, :].reshape(128, LANES), 1, 0) for b in range(4)
    ]
    cell = iota((1, 512), 1)
    at = cell & 255
    source = ((at * 2731) >> 16) * 24 + at + (cell >> 8) * 24
    source = jnp.where(at < 192, source, -1)
    move = (iota((384, 512), 0) == source).astype(BF16)
    sorted_rows = dot(jnp.concatenate(blocks[:3], axis=1).astype(BF16), move, 1, 0)
    tag = jnp.where(iota((128, 256), 1) >= 192, jnp.concatenate([blocks[3]] * 2, axis=1), 0.0)
    for core in range(2):
        half = (sorted_rows[:, 256 * core : 256 * core + 256] + tag).astype(BF16)
        for x in range(4):
            rows[2 * x + core] = half[32 * x : 32 * x + 32]
    wait(copies)


def land_body(got, out):
    total = None
    to = iota((1, 384), 1)
    for c in range(2):
        flat = got[:, 16 * c : 16 * c + 16, :].reshape(128, 256)
        where = flat[:, 192:193].astype(F32) == iota((128, 128), 1).astype(F32)
        rows = dot(where.astype(BF16), flat, 0, 0).astype(BF16)
        first, second = to - 128 * c, to - 128 - 64 * c
        source = jnp.where(
            (first >= 0) & (first < 128), first, jnp.where((second >= 128) & (second < 192), second, -1)
        )
        part = dot(rows, (iota((256, 384), 0) == source).astype(BF16), 1, 0)
        total = part if total is None else total + part
    total = total.astype(BF16)
    for y in range(8):
        out[y] = total


def forward_body(
    frame, band, query_h, key_h, value_h, b1, b2, b4, l1, l2, l4, prob_h, norm_h, score_h,
    query, key, pairs, later, prob, norm, score, sems
):
    moves = [(query_h, query), (key_h, key)]
    moves += [(b.at[:, :384], pairs.at[i]) for i, b in enumerate((b1, b2, b4))]
    moves += [(b, later.at[i]) for i, b in enumerate((l1, l2, l4))]
    wait(started(moves, sems))
    spread = jnp.abs(iota((128, 128), 0) - iota((128, 128), 1))
    f = frame[0]
    limits = [
        None,
        jnp.where(f >= 1, 128, 0),
        jnp.where(f >= 2, band[0, 0], 0),
        jnp.where(f >= 4, band[0, 1], 0),
    ]
    for h in range(3):
        q = query[:, lanes(h)]
        parts = []
        for i, limit in enumerate(limits):
            keys = key[:, lanes(h)] if i == 0 else pairs[i - 1, :, lanes(h)]
            s = dot(keys, q, 1, 1) * SCALE
            parts.append(s if limit is None else jnp.where(spread < limit, s, NEG_FILL))
        s = jnp.concatenate(parts, axis=0)
        top = jnp.max(s, axis=0, keepdims=True)
        w = jnp.exp(s - top)
        total = jnp.sum(w, axis=0, keepdims=True)
        prob[h] = w / total
        norm[:, lanes(h)] = jnp.broadcast_to(top + jnp.log(total), (8, 128))
        for i in range(3):
            score[3 * i + h] = dot(key[:, lanes(h)], later[i, :, lanes(h)], 1, 1) * SCALE
    wait(started(((prob, prob_h), (norm, norm_h), (score, score_h)), sems))


def parts_of(value):
    high = value.astype(BF16)
    rest = value - high.astype(F32)
    middle = rest.astype(BF16)
    return high, middle, (rest - middle.astype(F32)).astype(BF16)


def project_body(
    frame, rows, o0, o1, o2, o3, key_h, value_h, b1, b2, b4, prob_h, norm_h,
    mine, yours, keys, values, prob, norm, weight, sems
):
    x, core = (frame[0] >> 1) & 3, frame[0] & 1
    moves = []
    for turn, piece in enumerate((o0, o1, o2, o3)):
        to_x = (x + 4 - turn) & 3
        for h in range(3):
            moves.append((piece.at[:, 24 * h : 24 * h + 24, :], weight.at[:, to_x, :, lanes(h)]))
    moves += [(key_h, keys.at[0]), (value_h, values.at[0]), (prob_h, prob), (norm_h, norm)]
    for i, pair in enumerate((b1, b2, b4)):
        moves += [(pair.at[:, :384], keys.at[i + 1]), (pair.at[:, 384:], values.at[i + 1])]
    copies = started(moves, sems)
    wait(copies[:12])
    low = (iota((128, 128), 1) < 64).astype(F32).astype(BF16)
    high = (iota((128, 128), 1) >= 64).astype(F32).astype(BF16)
    total = None
    for y in range(8):
        block = rows[y]
        both = [
            jnp.concatenate([block[:, lanes(c)], block[:, 256:] * side], axis=1)
            for c, side in enumerate((low, high))
        ]
        block = weight[2 * y : 2 * y + 2].reshape(192, 384)
        block = jnp.concatenate([block, block[128:]], axis=0)
        part = dot(jnp.concatenate(both, axis=0), block, 1, 0)
        total = part if total is None else total + part
    mine[...] = jnp.where(core == 0, total[:128], total[128:])
    yours[...] = jnp.where(core == 0, total[128:], total[:128])
    wait(copies[12:])


def finish_body(band, mine, other, values, prob, norm, parcel, row_dot):
    grad = (mine[...] + other[...]).astype(BF16)
    parcel[:128, :] = grad
    dots = []
    for h in range(3):
        g = grad[:, lanes(h)]
        whole = jnp.zeros((1, 128), F32)
        for i in range(4):
            p = prob[h, 128 * i : 128 * i + 128].astype(BF16).astype(F32)
            whole = whole + jnp.sum(p * dot(values[i, :, lanes(h)], g, 1, 1), axis=0, keepdims=True)
        dots.append(whole)
    dots = jnp.concatenate(dots, axis=1)
    row_dot[...] = jnp.broadcast_to(dots, (8, 384))
    bands = [jnp.full((1, 384), band[0, i], jnp.int32).astype(F32) for i in range(2)]
    stack = [v.astype(F32) for v in parts_of(norm[:1]) + parts_of(dots)] + bands
    parcel[128:, :] = jnp.concatenate(stack, axis=0).astype(BF16)


def own_body(
    parcel, row_dot, prob, query_h, keys, values, l1, l2, l4, score_h,
    grad_query, key_part, value_part, later, score, query, sems
):
    moves = [(query_h, query), (score_h, score)]
    moves += [(b, later.at[i]) for i, b in enumerate((l1, l2, l4))]
    copies = started(moves, sems)
    for h in range(3):
        g = parcel[:128, lanes(h)]
        total = None
        for i in range(4):
            p = prob[h, 128 * i : 128 * i + 128]
            s = p * (dot(values[i, :, lanes(h)], g, 1, 1) - row_dot[:1, lanes(h)])
            s = s.astype(BF16)
            part = dot(s, keys[i, :, lanes(h)], 0, 0)
            total = part if total is None else total + part
            if i == 0:
                if h == 0:
                    wait(copies[:1])
                key_part[:, lanes(h)] = dot(s, query[:, lanes(h)], 1, 0)
                value_part[:, lanes(h)] = dot(p.astype(BF16), g, 1, 0)
        grad_query[:, lanes(h)] = (SCALE * total).astype(BF16)
    wait(copies[1:])


def later_body(frame, a1, a2, a4, later, score, values, key_part, value_part, grad_key, grad_value):
    spread = jnp.abs(iota((128, 128), 0) - iota((128, 128), 1)).astype(F32)
    for h in range(3):
        keys, vals = key_part[:, lanes(h)], value_part[:, lanes(h)]
        for i, (d, box) in enumerate(((1, a1), (2, a2), (4, a4))):
            extra = box[128:, lanes(h)].astype(F32)
            norm = extra[0:1] + extra[1:2] + extra[2:3]
            row_dot = extra[3:4] + extra[4:5] + extra[5:6]
            limit = jnp.full((1, 128), 128.0, F32) if d == 1 else extra[5 + d // 2 : 6 + d // 2]
            limit = jnp.where(frame[0] + d < 128, limit, 0.0)
            p = jnp.where(spread < limit, jnp.exp(score[3 * i + h] - norm), 0.0)
            g = box[:128, lanes(h)]
            s = (p * (dot(values[0, :, lanes(h)], g, 1, 1) - row_dot)).astype(BF16)
            keys = keys + dot(s, later[i, :, lanes(h)], 1, 0)
            vals = vals + dot(p.astype(BF16), g, 1, 0)
        grad_key[:, lanes(h)] = (SCALE * keys).astype(BF16)
        grad_value[:, lanes(h)] = vals.astype(BF16)


def step(
    grad_out, out_weight, row_owner, row_position, query_rows, key_rows, value_rows, band_widths
):
    frame = lax.axis_index(SEQ).reshape(1)

    packed, pair = call(
        pack_body,
        [((16, 104, LANES), BF16), ((128, 768), BF16)],
        "s" + "h" * 6 + "vv",
        (frame, row_owner[None], row_position[None], grad_out, out_weight.T, key_rows, value_rows),
        13_000_000,
        [((1, 128), jnp.int32), ((1, 128), jnp.int32), ((128, 384), BF16), ((24, 384), BF16)],
        6,
    )
    got = exchange(packed, "z")
    pairs, later = [], []
    for d in DISTANCES[1:]:
        pairs.append(shifted(pair, d))
    for d in DISTANCES[1:]:
        later.append(shifted(query_rows, -d))
    got, *later = lax.optimization_barrier((got, *later))
    own, rows = call(split_body, [((16, 72, LANES), BF16), ((8, 32, 256), BF16)], "vhv", (got,), 70_000_000, (), 1)
    rows = exchange(rows, ("x", "core"))
    (rows,) = call(land_body, [((8, 128, 384), BF16)], "vv", (rows,), 13_000_000)
    rows = exchange(rows, "head")

    right = turned(own, "x", 1)
    left = turned(own, "x", -1)
    far = turned(right, "x", 1)
    prob, norm, score = call(
        forward_body,
        [((3, 512, 128), F32), ((8, 384), F32), ((9, 128, 128), F32)],
        "ss" + "h" * 12,
        (frame, band_widths, query_rows, key_rows, value_rows, *pairs, *later),
        90_000_000,
        [((128, 384), BF16), ((128, 384), BF16), ((3, 128, 384), BF16), ((3, 128, 384), BF16)]
        + [((3, 512, 128), F32), ((8, 384), F32), ((9, 128, 128), F32)],
        8,
    )
    rows, far, left, prob, norm, score = lax.optimization_barrier((rows, far, left, prob, norm, score))

    mine, yours, keys, values, prob, norm = call(
        project_body,
        [((128, 384), F32)] * 2 + [((4, 128, 384), BF16)] * 2 + [((3, 512, 128), F32), ((8, 384), F32)],
        "sv" + "h" * 11 + "v" * 6,
        (frame, rows, own, right, far, left, key_rows, value_rows, *pairs, prob, norm),
        350_000_000,
        [((16, 4, 24, 384), BF16)],
        22,
    )
    other = turned(yours, "core", 1)
    parcel, row_dot = call(
        finish_body,
        [((136, 384), BF16), ((8, 384), F32)],
        "s" + "v" * 7,
        (band_widths, mine, other, values, prob, norm),
        50_000_000,
    )
    boxes = []
    for d in DISTANCES[1:]:
        boxes.append(shifted(parcel, -d))
    grad_query, key_part, value_part, later, score = call(
        own_body,
        [((128, 384), BF16), ((128, 384), F32), ((128, 384), F32), ((3, 128, 384), BF16), ((9, 128, 128), F32)],
        "vvvhvvhhhh" + "v" * 5,
        (parcel, row_dot, prob, query_rows, keys, values, *later, score),
        120_000_000,
        [((128, 384), BF16)],
        5,
    )
    grad_key, grad_value = call(
        later_body,
        [((128, 384), BF16), ((128, 384), BF16)],
        "s" + "v" * 10,
        (frame, *boxes, later, score, values, key_part, value_part),
        120_000_000,
    )
    return grad_query, grad_key, grad_value


def solution(mesh):
    grid = mesh.devices.reshape(tuple(SIZES.values()) + (mesh.shape["head"],))
    fine = Mesh(grid, tuple(SIZES) + ("head",))
    return jax.shard_map(
        step,
        mesh=fine,
        in_specs=(
            P(SEQ, "head"),
            P("head", SEQ),
            P(SEQ),
            P(SEQ),
            P(SEQ, "head"),
            P(SEQ, "head"),
            P(SEQ, "head"),
            P(SEQ, None),
        ),
        out_specs=(P(SEQ, "head"), P(SEQ, "head"), P(SEQ, "head")),
        check_vma=False,
    )
```

```python
import functools

import jax
import jax.numpy as jnp
from jax import lax
from jax.experimental import pallas as pl
from jax.experimental.pallas import tpu as pltpu
from jax.sharding import Mesh
from jax.sharding import PartitionSpec as P


HEAD_DIM = 128
LANES = 128
DISTANCES = (0, 1, 2, 4)
NEG_FILL = -1e30
SEQ = ("z", "x", "core")
SIZES = {"z": 16, "x": 4, "core": 2}
F32 = jnp.float32
BF16 = jnp.bfloat16
SCALE = HEAD_DIM ** (-0.5)


def shifted(value, by):
    peers = lax.axis_size(SEQ)
    pairs = [(i, i + by) for i in range(peers) if 0 <= i + by < peers]
    return lax.ppermute(value, SEQ, pairs)


def turned(value, axis, by):
    peers = lax.axis_size(axis)
    return lax.ppermute(value, axis, [(i, (i + by) % peers) for i in range(peers)])


def exchange(value, axis):
    return lax.all_to_all(value, axis, split_axis=0, concat_axis=0, tiled=True)


def dot(a, b, left, right):
    return lax.dot_general(a, b, (((left,), (right,)), ((), ())), preferred_element_type=F32)


SPACES = {"s": pltpu.SMEM, "v": pltpu.VMEM, "h": pltpu.HBM}


def call(body, outs, spaces, args, flops, scratch=(), copies=0):
    specs = [pl.BlockSpec(memory_space=SPACES[c]) for c in spaces]
    size = sum(a.size * a.dtype.itemsize for a in args)
    size += sum(int(jnp.dtype(t).itemsize) * functools.reduce(lambda m, n: m * n, s) for s, t in outs)
    args = [pltpu.with_memory_space_constraint(a, pltpu.HBM) if c == "h" else a for a, c in zip(args, spaces)]
    scratch = [pltpu.VMEM(shape, kind) for shape, kind in scratch]
    if copies:
        scratch.append(pltpu.SemaphoreType.DMA((copies,)))
    return pl.pallas_call(
        body,
        out_shape=[
            pltpu.HBM(s, t) if c == "h" else jax.ShapeDtypeStruct(s, t)
            for (s, t), c in zip(outs, spaces[len(args) :])
        ],
        in_specs=specs[: len(args)],
        out_specs=specs[len(args) :],
        scratch_shapes=scratch,
        cost_estimate=pl.CostEstimate(flops=flops, bytes_accessed=size, transcendentals=0),
        compiler_params=pltpu.CompilerParams(vmem_limit_bytes=8 * 2**20),
    )(*args)


def started(pairs, sems):
    copies = [pltpu.make_async_copy(a, b, sems.at[i]) for i, (a, b) in enumerate(pairs)]
    for copy in copies:
        copy.start()
    return copies


def wait(copies):
    for copy in copies:
        copy.wait()


def iota(shape, dim):
    return lax.broadcasted_iota(jnp.int32, shape, dim)


def lanes(h):
    return slice(h * LANES, (h + 1) * LANES)


def pack_body(frame, owner_h, place_h, grad_h, weight_h, key_h, value_h, out, pair, owner, place, grad, weight, sems):
    moves = ((owner_h, owner), (place_h, place), (grad_h, grad), (weight_h, weight))
    moves += ((key_h, pair.at[:, :384]), (value_h, pair.at[:, 384:]))
    copies = started(moves, sems)
    wait(copies[:4])
    pick = iota((128, 128), 0) == owner[...]
    where = jnp.sum(jnp.where(pick, place[...].astype(F32), 0.0), axis=1, keepdims=True)
    where = jnp.broadcast_to(where, (128, LANES)).astype(BF16)
    rows = dot(pick.astype(BF16), grad[...], 1, 0).astype(BF16)
    for h in range(3):
        piece = weight[:, lanes(h)]
        for z in range(16):
            out[z, 24 * h : 24 * h + 24, :] = piece
            out[z, 72 + 8 * h : 80 + 8 * h, :] = rows[8 * z : 8 * z + 8, lanes(h)]
    for z in range(16):
        out[z, 96:104, :] = where[8 * z : 8 * z + 8]
    wait(copies[4:])


def split_body(got, weight, rows, sems):
    copies = started(((got.at[:, :72, :], weight),), sems)
    row, col = iota((128, 128), 0), iota((128, 128), 1)
    order = (col == (row & 15) * 8 + (row >> 4)).astype(BF16)
    blocks = [
        dot(order, got[:, 72 + 8 * b : 80 + 8 * b, :].reshape(128, LANES), 1, 0) for b in range(4)
    ]
    cell = iota((1, 512), 1)
    at = cell & 255
    source = ((at * 2731) >> 16) * 24 + at + (cell >> 8) * 24
    source = jnp.where(at < 192, source, -1)
    move = (iota((384, 512), 0) == source).astype(BF16)
    sorted_rows = dot(jnp.concatenate(blocks[:3], axis=1).astype(BF16), move, 1, 0)
    tag = jnp.where(iota((128, 256), 1) >= 192, jnp.concatenate([blocks[3]] * 2, axis=1), 0.0)
    for core in range(2):
        half = (sorted_rows[:, 256 * core : 256 * core + 256] + tag).astype(BF16)
        for x in range(4):
            rows[2 * x + core] = half[32 * x : 32 * x + 32]
    wait(copies)


def land_body(got, out):
    total = None
    to = iota((1, 384), 1)
    for c in range(2):
        flat = got[:, 16 * c : 16 * c + 16, :].reshape(128, 256)
        where = flat[:, 192:193].astype(F32) == iota((128, 128), 1).astype(F32)
        rows = dot(where.astype(BF16), flat, 0, 0).astype(BF16)
        first, second = to - 128 * c, to - 128 - 64 * c
        source = jnp.where(
            (first >= 0) & (first < 128), first, jnp.where((second >= 128) & (second < 192), second, -1)
        )
        part = dot(rows, (iota((256, 384), 0) == source).astype(BF16), 1, 0)
        total = part if total is None else total + part
    total = total.astype(BF16)
    for y in range(8):
        out[y] = total


def forward_body(
    frame, band, query_h, key_h, value_h, b1, b2, b4, l1, l2, l4, prob_h, norm_h, score_h,
    query, key, pairs, later, prob, norm, score, sems
):
    moves = [(query_h, query), (key_h, key)]
    moves += [(b.at[:, :384], pairs.at[i]) for i, b in enumerate((b1, b2, b4))]
    moves += [(b, later.at[i]) for i, b in enumerate((l1, l2, l4))]
    wait(started(moves, sems))
    spread = jnp.abs(iota((128, 128), 0) - iota((128, 128), 1))
    f = frame[0]
    limits = [
        None,
        jnp.where(f >= 1, 128, 0),
        jnp.where(f >= 2, band[0, 0], 0),
        jnp.where(f >= 4, band[0, 1], 0),
    ]
    for h in range(3):
        q = query[:, lanes(h)]
        parts = []
        for i, limit in enumerate(limits):
            keys = key[:, lanes(h)] if i == 0 else pairs[i - 1, :, lanes(h)]
            s = dot(keys, q, 1, 1) * SCALE
            parts.append(s if limit is None else jnp.where(spread < limit, s, NEG_FILL))
        s = jnp.concatenate(parts, axis=0)
        top = jnp.max(s, axis=0, keepdims=True)
        w = jnp.exp(s - top)
        total = jnp.sum(w, axis=0, keepdims=True)
        prob[h] = w / total
        norm[:, lanes(h)] = jnp.broadcast_to(top + jnp.log(total), (8, 128))
        for i in range(3):
            score[3 * i + h] = dot(key[:, lanes(h)], later[i, :, lanes(h)], 1, 1) * SCALE
    wait(started(((prob, prob_h), (norm, norm_h), (score, score_h)), sems))


def parts_of(value):
    high = value.astype(BF16)
    rest = value - high.astype(F32)
    middle = rest.astype(BF16)
    return high, middle, (rest - middle.astype(F32)).astype(BF16)


def project_body(
    frame, rows, o0, o1, o2, o3, key_h, value_h, b1, b2, b4, prob_h, norm_h, query_h, l1, l2, l4, score_h,
    mine, yours, keys, values, prob, norm, query, later, score, weight, sems
):
    x, core = (frame[0] >> 1) & 3, frame[0] & 1
    moves = []
    for turn, piece in enumerate((o0, o1, o2, o3)):
        to_x = (x + 4 - turn) & 3
        for h in range(3):
            moves.append((piece.at[:, 24 * h : 24 * h + 24, :], weight.at[:, to_x, :, lanes(h)]))
    moves += [(key_h, keys.at[0]), (value_h, values.at[0]), (prob_h, prob), (norm_h, norm)]
    for i, pair in enumerate((b1, b2, b4)):
        moves += [(pair.at[:, :384], keys.at[i + 1]), (pair.at[:, 384:], values.at[i + 1])]
    moves += [(query_h, query), (score_h, score)]
    moves += [(b, later.at[i]) for i, b in enumerate((l1, l2, l4))]
    copies = started(moves, sems)
    wait(copies[:12])
    low = (iota((128, 128), 1) < 64).astype(F32).astype(BF16)
    high = (iota((128, 128), 1) >= 64).astype(F32).astype(BF16)
    total = None
    for y in range(8):
        block = rows[y]
        both = [
            jnp.concatenate([block[:, lanes(c)], block[:, 256:] * side], axis=1)
            for c, side in enumerate((low, high))
        ]
        block = weight[2 * y : 2 * y + 2].reshape(192, 384)
        block = jnp.concatenate([block, block[128:]], axis=0)
        part = dot(jnp.concatenate(both, axis=0), block, 1, 0)
        total = part if total is None else total + part
    mine[...] = jnp.where(core == 0, total[:128], total[128:])
    yours[...] = jnp.where(core == 0, total[128:], total[:128])
    wait(copies[12:])


def finish_body(band, mine, other, values, prob, norm, parcel, row_dot):
    grad = (mine[...] + other[...]).astype(BF16)
    parcel[:128, :] = grad
    dots = []
    for h in range(3):
        g = grad[:, lanes(h)]
        whole = jnp.zeros((1, 128), F32)
        for i in range(4):
            p = prob[h, 128 * i : 128 * i + 128].astype(BF16).astype(F32)
            whole = whole + jnp.sum(p * dot(values[i, :, lanes(h)], g, 1, 1), axis=0, keepdims=True)
        dots.append(whole)
    dots = jnp.concatenate(dots, axis=1)
    row_dot[...] = jnp.broadcast_to(dots, (8, 384))
    bands = [jnp.full((1, 384), band[0, i], jnp.int32).astype(F32) for i in range(2)]
    stack = [v.astype(F32) for v in parts_of(norm[:1]) + parts_of(dots)] + bands
    parcel[128:, :] = jnp.concatenate(stack, axis=0).astype(BF16)


def own_body(
    parcel, row_dot, prob, query, keys, values, grad_query, key_part, value_part
):
    for h in range(3):
        g = parcel[:128, lanes(h)]
        total = None
        for i in range(4):
            p = prob[h, 128 * i : 128 * i + 128]
            s = p * (dot(values[i, :, lanes(h)], g, 1, 1) - row_dot[:1, lanes(h)])
            s = s.astype(BF16)
            part = dot(s, keys[i, :, lanes(h)], 0, 0)
            total = part if total is None else total + part
            if i == 0:
                key_part[:, lanes(h)] = dot(s, query[:, lanes(h)], 1, 0)
                value_part[:, lanes(h)] = dot(p.astype(BF16), g, 1, 0)
        grad_query[:, lanes(h)] = (SCALE * total).astype(BF16)


def later_body(frame, a1, a2, a4, later, score, values, key_part, value_part, grad_key, grad_value):
    spread = jnp.abs(iota((128, 128), 0) - iota((128, 128), 1)).astype(F32)
    for h in range(3):
        keys, vals = key_part[:, lanes(h)], value_part[:, lanes(h)]
        for i, (d, box) in enumerate(((1, a1), (2, a2), (4, a4))):
            extra = box[128:, lanes(h)].astype(F32)
            norm = extra[0:1] + extra[1:2] + extra[2:3]
            row_dot = extra[3:4] + extra[4:5] + extra[5:6]
            limit = jnp.full((1, 128), 128.0, F32) if d == 1 else extra[5 + d // 2 : 6 + d // 2]
            limit = jnp.where(frame[0] + d < 128, limit, 0.0)
            p = jnp.where(spread < limit, jnp.exp(score[3 * i + h] - norm), 0.0)
            g = box[:128, lanes(h)]
            s = (p * (dot(values[0, :, lanes(h)], g, 1, 1) - row_dot)).astype(BF16)
            keys = keys + dot(s, later[i, :, lanes(h)], 1, 0)
            vals = vals + dot(p.astype(BF16), g, 1, 0)
        grad_key[:, lanes(h)] = (SCALE * keys).astype(BF16)
        grad_value[:, lanes(h)] = vals.astype(BF16)


def step(
    grad_out, out_weight, row_owner, row_position, query_rows, key_rows, value_rows, band_widths
):
    frame = lax.axis_index(SEQ).reshape(1)

    packed, pair = call(
        pack_body,
        [((16, 104, LANES), BF16), ((128, 768), BF16)],
        "s" + "h" * 6 + "vv",
        (frame, row_owner[None], row_position[None], grad_out, out_weight.T, key_rows, value_rows),
        13_000_000,
        [((1, 128), jnp.int32), ((1, 128), jnp.int32), ((128, 384), BF16), ((24, 384), BF16)],
        6,
    )
    got = exchange(packed, "z")
    pairs, later = [], []
    for d in DISTANCES[1:]:
        pairs.append(shifted(pair, d))
    for d in DISTANCES[1:]:
        later.append(shifted(query_rows, -d))
    got, later[0] = lax.optimization_barrier((got, later[0]))
    own, rows = call(split_body, [((16, 72, LANES), BF16), ((8, 32, 256), BF16)], "vhv", (got,), 70_000_000, (), 1)
    rows = exchange(rows, ("x", "core"))
    (rows,) = call(land_body, [((8, 128, 384), BF16)], "vv", (rows,), 13_000_000)
    rows = exchange(rows, "head")

    right = turned(own, "x", 1)
    left = turned(own, "x", -1)
    far = turned(right, "x", 1)
    prob, norm, score = call(
        forward_body,
        [((3, 512, 128), F32), ((8, 384), F32), ((9, 128, 128), F32)],
        "ss" + "h" * 12,
        (frame, band_widths, query_rows, key_rows, value_rows, *pairs, *later),
        90_000_000,
        [((128, 384), BF16), ((128, 384), BF16), ((3, 128, 384), BF16), ((3, 128, 384), BF16)]
        + [((3, 512, 128), F32), ((8, 384), F32), ((9, 128, 128), F32)],
        8,
    )
    rows, far, left, prob, norm, score = lax.optimization_barrier((rows, far, left, prob, norm, score))

    mine, yours, keys, values, prob, norm, query, later, score = call(
        project_body,
        [((128, 384), F32)] * 2
        + [((4, 128, 384), BF16)] * 2
        + [((3, 512, 128), F32), ((8, 384), F32), ((128, 384), BF16), ((3, 128, 384), BF16), ((9, 128, 128), F32)],
        "sv" + "h" * 16 + "v" * 9,
        (frame, rows, own, right, far, left, key_rows, value_rows, *pairs, prob, norm, query_rows, *later, score),
        350_000_000,
        [((16, 4, 24, 384), BF16)],
        27,
    )
    other = turned(yours, "core", 1)
    parcel, row_dot = call(
        finish_body,
        [((136, 384), BF16), ((8, 384), F32)],
        "s" + "v" * 7,
        (band_widths, mine, other, values, prob, norm),
        50_000_000,
    )
    boxes = []
    for d in DISTANCES[1:]:
        boxes.append(shifted(parcel, -d))
    grad_query, key_part, value_part = call(
        own_body,
        [((128, 384), BF16), ((128, 384), F32), ((128, 384), F32)],
        "v" * 9,
        (parcel, row_dot, prob, query, keys, values),
        120_000_000,
    )
    grad_key, grad_value = call(
        later_body,
        [((128, 384), BF16), ((128, 384), BF16)],
        "s" + "v" * 10,
        (frame, *boxes, later, score, values, key_part, value_part),
        120_000_000,
    )
    return grad_query, grad_key, grad_value


def solution(mesh):
    grid = mesh.devices.reshape(tuple(SIZES.values()) + (mesh.shape["head"],))
    fine = Mesh(grid, tuple(SIZES) + ("head",))
    return jax.shard_map(
        step,
        mesh=fine,
        in_specs=(
            P(SEQ, "head"),
            P("head", SEQ),
            P(SEQ),
            P(SEQ),
            P(SEQ, "head"),
            P(SEQ, "head"),
            P(SEQ, "head"),
            P(SEQ, None),
        ),
        out_specs=(P(SEQ, "head"), P(SEQ, "head"), P(SEQ, "head")),
        check_vma=False,
    )
```

```python
import functools

import jax
import jax.numpy as jnp
from jax import lax
from jax.experimental import pallas as pl
from jax.experimental.pallas import tpu as pltpu
from jax.sharding import Mesh
from jax.sharding import PartitionSpec as P


HEAD_DIM = 128
LANES = 128
DISTANCES = (0, 1, 2, 4)
NEG_FILL = -1e30
SEQ = ("z", "x", "core")
SIZES = {"z": 16, "x": 4, "core": 2}
F32 = jnp.float32
BF16 = jnp.bfloat16
SCALE = HEAD_DIM ** (-0.5)


def shifted(value, by):
    peers = lax.axis_size(SEQ)
    pairs = [(i, i + by) for i in range(peers) if 0 <= i + by < peers]
    return lax.ppermute(value, SEQ, pairs)


def turned(value, axis, by):
    peers = lax.axis_size(axis)
    return lax.ppermute(value, axis, [(i, (i + by) % peers) for i in range(peers)])


def exchange(value, axis):
    return lax.all_to_all(value, axis, split_axis=0, concat_axis=0, tiled=True)


def dot(a, b, left, right):
    return lax.dot_general(a, b, (((left,), (right,)), ((), ())), preferred_element_type=F32)


SPACES = {"s": pltpu.SMEM, "v": pltpu.VMEM, "h": pltpu.HBM}


def call(body, outs, spaces, args, flops, scratch=(), copies=0):
    specs = [pl.BlockSpec(memory_space=SPACES[c]) for c in spaces]
    size = sum(a.size * a.dtype.itemsize for a in args)
    size += sum(int(jnp.dtype(t).itemsize) * functools.reduce(lambda m, n: m * n, s) for s, t in outs)
    args = [pltpu.with_memory_space_constraint(a, pltpu.HBM) if c == "h" else a for a, c in zip(args, spaces)]
    scratch = [pltpu.VMEM(shape, kind) for shape, kind in scratch]
    if copies:
        scratch.append(pltpu.SemaphoreType.DMA((copies,)))
    return pl.pallas_call(
        body,
        out_shape=[
            pltpu.HBM(s, t) if c == "h" else jax.ShapeDtypeStruct(s, t)
            for (s, t), c in zip(outs, spaces[len(args) :])
        ],
        in_specs=specs[: len(args)],
        out_specs=specs[len(args) :],
        scratch_shapes=scratch,
        cost_estimate=pl.CostEstimate(flops=flops, bytes_accessed=size, transcendentals=0),
        compiler_params=pltpu.CompilerParams(vmem_limit_bytes=8 * 2**20),
    )(*args)


def started(pairs, sems):
    copies = [pltpu.make_async_copy(a, b, sems.at[i]) for i, (a, b) in enumerate(pairs)]
    for copy in copies:
        copy.start()
    return copies


def wait(copies):
    for copy in copies:
        copy.wait()


def iota(shape, dim):
    return lax.broadcasted_iota(jnp.int32, shape, dim)


def lanes(h):
    return slice(h * LANES, (h + 1) * LANES)


def pack_body(frame, owner_h, place_h, grad_h, weight_h, key_h, value_h, out, pair, owner, place, grad, weight, sems):
    moves = ((owner_h, owner), (place_h, place), (grad_h, grad), (weight_h, weight))
    moves += ((key_h, pair.at[:, :384]), (value_h, pair.at[:, 384:]))
    copies = started(moves, sems)
    wait(copies[:4])
    pick = iota((128, 128), 0) == owner[...]
    where = jnp.sum(jnp.where(pick, place[...].astype(F32), 0.0), axis=1, keepdims=True)
    where = jnp.broadcast_to(where, (128, LANES)).astype(BF16)
    rows = dot(pick.astype(BF16), grad[...], 1, 0).astype(BF16)
    for h in range(3):
        piece = weight[:, lanes(h)]
        for z in range(16):
            out[z, 24 * h : 24 * h + 24, :] = piece
            out[z, 80 + 8 * h : 88 + 8 * h, :] = rows[8 * z : 8 * z + 8, lanes(h)]
    for z in range(16):
        out[z, 72:80, :] = where[8 * z : 8 * z + 8]
    wait(copies[4:])


def split_body(got, weight, rows, sems):
    copies = started(((got.at[:, :80, :], weight),), sems)
    row, col = iota((128, 128), 0), iota((128, 128), 1)
    order = (col == (row & 15) * 8 + (row >> 4)).astype(BF16)
    blocks = [
        dot(order, got[:, 80 + 8 * b : 88 + 8 * b, :].reshape(128, LANES), 1, 0) for b in range(3)
    ]
    cell = iota((1, 768), 1)
    core = (cell >= 384).astype(jnp.int32)
    at = cell - 384 * core
    place = jnp.where(at < 192, at, jnp.where(at >= 320, at - 192, -1))
    source = jnp.where(place >= 0, place + ((place * 2731) >> 16) * 24 + core * 24, -1)
    move = (iota((384, 768), 0) == source).astype(BF16)
    moved = dot(jnp.concatenate(blocks, axis=1).astype(BF16), move, 1, 0)
    for x in range(4):
        first, second = moved[32 * x : 32 * x + 16], moved[32 * x + 16 : 32 * x + 32]
        for c in range(2):
            begin = 3 * c
            block = [first[:, lanes(begin)], second[:, lanes(begin)]]
            block.append(first[:, lanes(begin + 1)] + second[:, lanes(begin + 2)])
            block = jnp.concatenate(block, axis=0).astype(BF16)
            for y in range(8):
                rows[y, 2 * x + c] = block
    wait(copies)


def forward_body(
    frame, band, query_h, key_h, value_h, b1, b2, b4, l1, l2, l4, prob_h, norm_h, score_h,
    query, key, pairs, later, prob, norm, score, sems
):
    moves = [(query_h, query), (key_h, key)]
    moves += [(b.at[:, :384], pairs.at[i]) for i, b in enumerate((b1, b2, b4))]
    moves += [(b, later.at[i]) for i, b in enumerate((l1, l2, l4))]
    wait(started(moves, sems))
    spread = jnp.abs(iota((128, 128), 0) - iota((128, 128), 1))
    f = frame[0]
    limits = [
        None,
        jnp.where(f >= 1, 128, 0),
        jnp.where(f >= 2, band[0, 0], 0),
        jnp.where(f >= 4, band[0, 1], 0),
    ]
    for h in range(3):
        q = query[:, lanes(h)]
        parts = []
        for i, limit in enumerate(limits):
            keys = key[:, lanes(h)] if i == 0 else pairs[i - 1, :, lanes(h)]
            s = dot(keys, q, 1, 1) * SCALE
            parts.append(s if limit is None else jnp.where(spread < limit, s, NEG_FILL))
        s = jnp.concatenate(parts, axis=0)
        top = jnp.max(s, axis=0, keepdims=True)
        w = jnp.exp(s - top)
        total = jnp.sum(w, axis=0, keepdims=True)
        prob[h] = w / total
        norm[:, lanes(h)] = jnp.broadcast_to(top + jnp.log(total), (8, 128))
        for i in range(3):
            score[3 * i + h] = dot(key[:, lanes(h)], later[i, :, lanes(h)], 1, 1) * SCALE
    wait(started(((prob, prob_h), (norm, norm_h), (score, score_h)), sems))


def parts_of(value):
    high = value.astype(BF16)
    rest = value - high.astype(F32)
    middle = rest.astype(BF16)
    return high, middle, (rest - middle.astype(F32)).astype(BF16)


def project_body(
    frame, rows, o0, o1, o2, o3, key_h, value_h, b1, b2, b4, prob_h, norm_h, query_h, l1, l2, l4, score_h,
    mine, yours, keys, values, prob, norm, query, later, score, weight, places, sems
):
    x, core = (frame[0] >> 1) & 3, frame[0] & 1
    moves = []
    for turn, piece in enumerate((o0, o1, o2, o3)):
        to_x = (x + 4 - turn) & 3
        for h in range(3):
            moves.append((piece.at[:, 24 * h : 24 * h + 24, :], weight.at[:, to_x, :, lanes(h)]))
        moves.append((piece.at[:, 72:80, :], places.at[to_x]))
    moves += [(key_h, keys.at[0]), (value_h, values.at[0]), (prob_h, prob), (norm_h, norm)]
    for i, pair in enumerate((b1, b2, b4)):
        moves += [(pair.at[:, :384], keys.at[i + 1]), (pair.at[:, 384:], values.at[i + 1])]
    moves += [(query_h, query), (score_h, score)]
    moves += [(b, later.at[i]) for i, b in enumerate((l1, l2, l4))]
    copies = started(moves, sems)
    wait(copies[:16])
    low = (iota((128, 128), 1) < 64).astype(F32).astype(BF16)
    high = (iota((128, 128), 1) >= 64).astype(F32).astype(BF16)
    total = None
    for y in range(8):
        rest = rows[y, :, 32:48, :].reshape(128, LANES)
        both = [
            jnp.concatenate([rows[y, :, 16 * c : 16 * c + 16, :].reshape(128, LANES), rest * side], axis=1)
            for c, side in enumerate((low, high))
        ]
        block = weight[2 * y : 2 * y + 2].reshape(192, 384)
        block = jnp.concatenate([block, block[128:]], axis=0)
        part = dot(jnp.concatenate(both, axis=0), block, 1, 0)
        total = part if total is None else total + part
    where = places[...].astype(F32).reshape(64, 8, LANES)
    for out, frame_core, half in (
        (mine, core, jnp.where(core == 0, total[:128], total[128:])),
        (yours, 1 - core, jnp.where(core == 0, total[128:], total[:128])),
    ):
        out[:128, :] = half
        at = jnp.sum(jnp.where(iota((64, 8, LANES), 1) == 2 * x + frame_core, where, 0.0), axis=1)
        tail = jnp.concatenate([at[48:], jnp.zeros((8, LANES), F32)], axis=0)
        out[128:, :] = jnp.concatenate([at[:24], at[24:48], tail], axis=1)
    wait(copies[16:])


def places_of(half):
    return jnp.concatenate([half[128:, lanes(0)], half[128:, lanes(1)], half[128:144, lanes(2)]], axis=0)


def finish_body(frame, band, mine, other, values, prob, norm, parcel, row_dot):
    core = frame[0] & 1
    packed = (mine[:128, :] + other[:128, :]).astype(BF16)
    own, far = places_of(mine), places_of(other)
    first, second = jnp.where(core == 0, own, far), jnp.where(core == 0, far, own)
    where = []
    for x in range(4):
        where += [first[16 * x : 16 * x + 16], second[16 * x : 16 * x + 16]]
    where = jnp.concatenate(where, axis=0) == iota((128, 128), 1).astype(F32)
    grad = dot(where.astype(F32).astype(BF16), packed, 0, 0).astype(BF16)
    parcel[:128, :] = grad
    dots = []
    for h in range(3):
        g = grad[:, lanes(h)]
        whole = jnp.zeros((1, 128), F32)
        for i in range(4):
            p = prob[h, 128 * i : 128 * i + 128].astype(BF16).astype(F32)
            whole = whole + jnp.sum(p * dot(values[i, :, lanes(h)], g, 1, 1), axis=0, keepdims=True)
        dots.append(whole)
    dots = jnp.concatenate(dots, axis=1)
    row_dot[...] = jnp.broadcast_to(dots, (8, 384))
    bands = [jnp.full((1, 384), band[0, i], jnp.int32).astype(F32) for i in range(2)]
    stack = [v.astype(F32) for v in parts_of(norm[:1]) + parts_of(dots)] + bands
    parcel[128:, :] = jnp.concatenate(stack, axis=0).astype(BF16)


def own_body(
    parcel, row_dot, prob, query, keys, values, grad_query, key_part, value_part
):
    for h in range(3):
        g = parcel[:128, lanes(h)]
        total = None
        for i in range(4):
            p = prob[h, 128 * i : 128 * i + 128]
            s = p * (dot(values[i, :, lanes(h)], g, 1, 1) - row_dot[:1, lanes(h)])
            s = s.astype(BF16)
            part = dot(s, keys[i, :, lanes(h)], 0, 0)
            total = part if total is None else total + part
            if i == 0:
                key_part[:, lanes(h)] = dot(s, query[:, lanes(h)], 1, 0)
                value_part[:, lanes(h)] = dot(p.astype(BF16), g, 1, 0)
        grad_query[:, lanes(h)] = (SCALE * total).astype(BF16)


def later_body(frame, a1, a2, a4, later, score, values, key_part, value_part, grad_key, grad_value):
    spread = jnp.abs(iota((128, 128), 0) - iota((128, 128), 1)).astype(F32)
    for h in range(3):
        keys, vals = key_part[:, lanes(h)], value_part[:, lanes(h)]
        for i, (d, box) in enumerate(((1, a1), (2, a2), (4, a4))):
            extra = box[128:, lanes(h)].astype(F32)
            norm = extra[0:1] + extra[1:2] + extra[2:3]
            row_dot = extra[3:4] + extra[4:5] + extra[5:6]
            limit = jnp.full((1, 128), 128.0, F32) if d == 1 else extra[5 + d // 2 : 6 + d // 2]
            limit = jnp.where(frame[0] + d < 128, limit, 0.0)
            p = jnp.where(spread < limit, jnp.exp(score[3 * i + h] - norm), 0.0)
            g = box[:128, lanes(h)]
            s = (p * (dot(values[0, :, lanes(h)], g, 1, 1) - row_dot)).astype(BF16)
            keys = keys + dot(s, later[i, :, lanes(h)], 1, 0)
            vals = vals + dot(p.astype(BF16), g, 1, 0)
        grad_key[:, lanes(h)] = (SCALE * keys).astype(BF16)
        grad_value[:, lanes(h)] = vals.astype(BF16)


def step(
    grad_out, out_weight, row_owner, row_position, query_rows, key_rows, value_rows, band_widths
):
    frame = lax.axis_index(SEQ).reshape(1)

    packed, pair = call(
        pack_body,
        [((16, 104, LANES), BF16), ((128, 768), BF16)],
        "s" + "h" * 6 + "vv",
        (frame, row_owner[None], row_position[None], grad_out, out_weight.T, key_rows, value_rows),
        13_000_000,
        [((1, 128), jnp.int32), ((1, 128), jnp.int32), ((128, 384), BF16), ((24, 384), BF16)],
        6,
    )
    got = exchange(packed, "z")
    pairs, later = [], []
    for d in DISTANCES[1:]:
        pairs.append(shifted(pair, d))
    for d in DISTANCES[1:]:
        later.append(shifted(query_rows, -d))
    got, later[0] = lax.optimization_barrier((got, later[0]))
    own, rows = call(
        split_body, [((16, 80, LANES), BF16), ((8, 8, 48, LANES), BF16)], "vhv", (got,), 100_000_000, (), 1
    )
    rows = exchange(rows.reshape(64, 48, LANES), ("head", "x", "core")).reshape(8, 8, 48, LANES)

    right = turned(own, "x", 1)
    left = turned(own, "x", -1)
    far = turned(right, "x", 1)
    prob, norm, score = call(
        forward_body,
        [((3, 512, 128), F32), ((8, 384), F32), ((9, 128, 128), F32)],
        "ss" + "h" * 12,
        (frame, band_widths, query_rows, key_rows, value_rows, *pairs, *later),
        90_000_000,
        [((128, 384), BF16), ((128, 384), BF16), ((3, 128, 384), BF16), ((3, 128, 384), BF16)]
        + [((3, 512, 128), F32), ((8, 384), F32), ((9, 128, 128), F32)],
        8,
    )
    rows, far, left, prob, norm, score = lax.optimization_barrier((rows, far, left, prob, norm, score))

    mine, yours, keys, values, prob, norm, query, later, score = call(
        project_body,
        [((152, 384), F32)] * 2
        + [((4, 128, 384), BF16)] * 2
        + [((3, 512, 128), F32), ((8, 384), F32), ((128, 384), BF16), ((3, 128, 384), BF16), ((9, 128, 128), F32)],
        "sv" + "h" * 16 + "v" * 9,
        (frame, rows, own, right, far, left, key_rows, value_rows, *pairs, prob, norm, query_rows, *later, score),
        350_000_000,
        [((16, 4, 24, 384), BF16), ((4, 16, 8, LANES), BF16)],
        31,
    )
    other = turned(yours, "core", 1)
    parcel, row_dot = call(
        finish_body,
        [((136, 384), BF16), ((8, 384), F32)],
        "ss" + "v" * 7,
        (frame, band_widths, mine, other, values, prob, norm),
        50_000_000,
    )
    boxes = []
    for d in DISTANCES[1:]:
        boxes.append(shifted(parcel, -d))
    grad_query, key_part, value_part = call(
        own_body,
        [((128, 384), BF16), ((128, 384), F32), ((128, 384), F32)],
        "v" * 9,
        (parcel, row_dot, prob, query, keys, values),
        120_000_000,
    )
    grad_key, grad_value = call(
        later_body,
        [((128, 384), BF16), ((128, 384), BF16)],
        "s" + "v" * 10,
        (frame, *boxes, later, score, values, key_part, value_part),
        120_000_000,
    )
    return grad_query, grad_key, grad_value


def solution(mesh):
    grid = mesh.devices.reshape(tuple(SIZES.values()) + (mesh.shape["head"],))
    fine = Mesh(grid, tuple(SIZES) + ("head",))
    return jax.shard_map(
        step,
        mesh=fine,
        in_specs=(
            P(SEQ, "head"),
            P("head", SEQ),
            P(SEQ),
            P(SEQ),
            P(SEQ, "head"),
            P(SEQ, "head"),
            P(SEQ, "head"),
            P(SEQ, None),
        ),
        out_specs=(P(SEQ, "head"), P(SEQ, "head"), P(SEQ, "head")),
        check_vma=False,
    )
```

```python
import functools

import jax
import jax.numpy as jnp
from jax import lax
from jax.experimental import pallas as pl
from jax.experimental.pallas import tpu as pltpu
from jax.sharding import Mesh
from jax.sharding import PartitionSpec as P


HEAD_DIM = 128
LANES = 128
DISTANCES = (0, 1, 2, 4)
NEG_FILL = -1e30
SEQ = ("z", "x", "core")
SIZES = {"z": 16, "x": 4, "core": 2}
F32 = jnp.float32
BF16 = jnp.bfloat16
SCALE = HEAD_DIM ** (-0.5)


def shifted(value, by):
    peers = lax.axis_size(SEQ)
    pairs = [(i, i + by) for i in range(peers) if 0 <= i + by < peers]
    return lax.ppermute(value, SEQ, pairs)


def turned(value, axis, by):
    peers = lax.axis_size(axis)
    return lax.ppermute(value, axis, [(i, (i + by) % peers) for i in range(peers)])


def exchange(value, axis):
    return lax.all_to_all(value, axis, split_axis=0, concat_axis=0, tiled=True)


def dot(a, b, left, right):
    return lax.dot_general(a, b, (((left,), (right,)), ((), ())), preferred_element_type=F32)


SPACES = {"s": pltpu.SMEM, "v": pltpu.VMEM, "h": pltpu.HBM}


def call(body, outs, spaces, args, flops, scratch=(), copies=0):
    specs = [pl.BlockSpec(memory_space=SPACES[c]) for c in spaces]
    size = sum(a.size * a.dtype.itemsize for a in args)
    size += sum(int(jnp.dtype(t).itemsize) * functools.reduce(lambda m, n: m * n, s) for s, t in outs)
    args = [pltpu.with_memory_space_constraint(a, pltpu.HBM) if c == "h" else a for a, c in zip(args, spaces)]
    scratch = [pltpu.VMEM(shape, kind) for shape, kind in scratch]
    if copies:
        scratch.append(pltpu.SemaphoreType.DMA((copies,)))
    return pl.pallas_call(
        body,
        out_shape=[
            pltpu.HBM(s, t) if c == "h" else jax.ShapeDtypeStruct(s, t)
            for (s, t), c in zip(outs, spaces[len(args) :])
        ],
        in_specs=specs[: len(args)],
        out_specs=specs[len(args) :],
        scratch_shapes=scratch,
        cost_estimate=pl.CostEstimate(flops=flops, bytes_accessed=size, transcendentals=0),
        compiler_params=pltpu.CompilerParams(vmem_limit_bytes=8 * 2**20),
    )(*args)


def started(pairs, sems):
    copies = [pltpu.make_async_copy(a, b, sems.at[i]) for i, (a, b) in enumerate(pairs)]
    for copy in copies:
        copy.start()
    return copies


def wait(copies):
    for copy in copies:
        copy.wait()


def iota(shape, dim):
    return lax.broadcasted_iota(jnp.int32, shape, dim)


def lanes(h):
    return slice(h * LANES, (h + 1) * LANES)


def pack_body(frame, owner_h, place_h, grad_h, weight_h, key_h, value_h, out, pair, owner, place, grad, weight, sems):
    moves = ((owner_h, owner), (place_h, place), (grad_h, grad), (weight_h, weight))
    moves += ((key_h, pair.at[:, :384]), (value_h, pair.at[:, 384:]))
    copies = started(moves, sems)
    wait(copies[:4])
    pick = iota((128, 128), 0) == owner[...]
    where = jnp.sum(jnp.where(pick, place[...].astype(F32), 0.0), axis=1, keepdims=True)
    where = jnp.broadcast_to(where, (128, LANES)).astype(BF16)
    rows = dot(pick.astype(BF16), grad[...], 1, 0).astype(BF16)
    for h in range(3):
        piece = weight[:, lanes(h)]
        for z in range(16):
            out[z, 24 * h : 24 * h + 24, :] = piece
            out[z, 80 + 8 * h : 88 + 8 * h, :] = rows[8 * z : 8 * z + 8, lanes(h)]
    for z in range(16):
        out[z, 72:80, :] = where[8 * z : 8 * z + 8]
    wait(copies[4:])


def split_body(got, weight, rows, sems):
    copies = started(((got.at[:, :80, :], weight),), sems)
    row, col = iota((128, 128), 0), iota((128, 128), 1)
    order = (col == (row & 15) * 8 + (row >> 4)).astype(BF16)
    blocks = [
        dot(order, got[:, 80 + 8 * b : 88 + 8 * b, :].reshape(128, LANES), 1, 0) for b in range(3)
    ]
    cell = iota((1, 768), 1)
    core = (cell >= 384).astype(jnp.int32)
    at = cell - 384 * core
    place = jnp.where(at < 192, at, jnp.where(at >= 320, at - 192, -1))
    source = jnp.where(place >= 0, place + ((place * 2731) >> 16) * 24 + core * 24, -1)
    move = (iota((384, 768), 0) == source).astype(BF16)
    moved = dot(jnp.concatenate(blocks, axis=1).astype(BF16), move, 1, 0)
    for x in range(4):
        first, second = moved[32 * x : 32 * x + 16], moved[32 * x + 16 : 32 * x + 32]
        for c in range(2):
            begin = 3 * c
            block = [first[:, lanes(begin)], second[:, lanes(begin)]]
            block.append(first[:, lanes(begin + 1)] + second[:, lanes(begin + 2)])
            block = jnp.concatenate(block, axis=0).astype(BF16)
            for y in range(8):
                rows[y, 2 * x + c] = block
    wait(copies)


def forward_body(
    frame, band, query_h, key_h, value_h, b1, b2, b4, l1, l2, l4, prob_h, norm_h, score_h,
    query, key, pairs, later, prob, norm, score, sems
):
    moves = [(query_h, query), (key_h, key)]
    moves += [(b.at[:, :384], pairs.at[i]) for i, b in enumerate((b1, b2, b4))]
    moves += [(b, later.at[i]) for i, b in enumerate((l1, l2, l4))]
    wait(started(moves, sems))
    spread = jnp.abs(iota((128, 128), 0) - iota((128, 128), 1))
    f = frame[0]
    limits = [
        None,
        jnp.where(f >= 1, 128, 0),
        jnp.where(f >= 2, band[0, 0], 0),
        jnp.where(f >= 4, band[0, 1], 0),
    ]
    for h in range(3):
        q = query[:, lanes(h)]
        parts = []
        for i, limit in enumerate(limits):
            keys = key[:, lanes(h)] if i == 0 else pairs[i - 1, :, lanes(h)]
            s = dot(keys, q, 1, 1) * SCALE
            parts.append(s if limit is None else jnp.where(spread < limit, s, NEG_FILL))
        s = jnp.concatenate(parts, axis=0)
        top = jnp.max(s, axis=0, keepdims=True)
        w = jnp.exp(s - top)
        total = jnp.sum(w, axis=0, keepdims=True)
        prob[h] = w / total
        norm[:, lanes(h)] = jnp.broadcast_to(top + jnp.log(total), (8, 128))
        for i in range(3):
            score[3 * i + h] = dot(key[:, lanes(h)], later[i, :, lanes(h)], 1, 1) * SCALE
    wait(started(((prob, prob_h), (norm, norm_h), (score, score_h)), sems))


def parts_of(value):
    high = value.astype(BF16)
    rest = value - high.astype(F32)
    middle = rest.astype(BF16)
    return high, middle, (rest - middle.astype(F32)).astype(BF16)


def project_body(
    frame, rows, o0, o1, o2, o3, key_h, value_h, b1, b2, b4, prob_h, norm_h,
    mine, yours, keys, values, prob, norm, weight, places, sems
):
    x, core = (frame[0] >> 1) & 3, frame[0] & 1
    moves = []
    for turn, piece in enumerate((o0, o1, o2, o3)):
        to_x = (x + 4 - turn) & 3
        for h in range(3):
            moves.append((piece.at[:, 24 * h : 24 * h + 24, :], weight.at[:, to_x, :, lanes(h)]))
        moves.append((piece.at[:, 72:80, :], places.at[to_x]))
    moves += [(key_h, keys.at[0]), (value_h, values.at[0]), (prob_h, prob), (norm_h, norm)]
    for i, pair in enumerate((b1, b2, b4)):
        moves += [(pair.at[:, :384], keys.at[i + 1]), (pair.at[:, 384:], values.at[i + 1])]
    copies = started(moves, sems)
    wait(copies[:16])
    low = (iota((128, 128), 1) < 64).astype(F32).astype(BF16)
    high = (iota((128, 128), 1) >= 64).astype(F32).astype(BF16)
    total = None
    for y in range(8):
        rest = rows[y, :, 32:48, :].reshape(128, LANES)
        both = [
            jnp.concatenate([rows[y, :, 16 * c : 16 * c + 16, :].reshape(128, LANES), rest * side], axis=1)
            for c, side in enumerate((low, high))
        ]
        block = weight[2 * y : 2 * y + 2].reshape(192, 384)
        block = jnp.concatenate([block, block[128:]], axis=0)
        part = dot(jnp.concatenate(both, axis=0), block, 1, 0)
        total = part if total is None else total + part
    where = places[...].astype(F32).reshape(64, 8, LANES)
    for out, frame_core, half in (
        (mine, core, jnp.where(core == 0, total[:128], total[128:])),
        (yours, 1 - core, jnp.where(core == 0, total[128:], total[:128])),
    ):
        out[:128, :] = half
        at = jnp.sum(jnp.where(iota((64, 8, LANES), 1) == 2 * x + frame_core, where, 0.0), axis=1)
        tail = jnp.concatenate([at[48:], jnp.zeros((8, LANES), F32)], axis=0)
        out[128:, :] = jnp.concatenate([at[:24], at[24:48], tail], axis=1)
    wait(copies[16:])


def places_of(half):
    return jnp.concatenate([half[128:, lanes(0)], half[128:, lanes(1)], half[128:144, lanes(2)]], axis=0)


def finish_body(
    frame, band, mine, other, values, prob, norm, query_h, l1, l2, l4, score_h,
    parcel, row_dot, query, later, score, sems
):
    moves = [(query_h, query), (score_h, score)]
    moves += [(b, later.at[i]) for i, b in enumerate((l1, l2, l4))]
    copies = started(moves, sems)
    core = frame[0] & 1
    packed = (mine[:128, :] + other[:128, :]).astype(BF16)
    own, far = places_of(mine), places_of(other)
    first, second = jnp.where(core == 0, own, far), jnp.where(core == 0, far, own)
    where = []
    for x in range(4):
        where += [first[16 * x : 16 * x + 16], second[16 * x : 16 * x + 16]]
    where = jnp.concatenate(where, axis=0) == iota((128, 128), 1).astype(F32)
    grad = dot(where.astype(F32).astype(BF16), packed, 0, 0).astype(BF16)
    parcel[:128, :] = grad
    dots = []
    for h in range(3):
        g = grad[:, lanes(h)]
        whole = jnp.zeros((1, 128), F32)
        for i in range(4):
            p = prob[h, 128 * i : 128 * i + 128].astype(BF16).astype(F32)
            whole = whole + jnp.sum(p * dot(values[i, :, lanes(h)], g, 1, 1), axis=0, keepdims=True)
        dots.append(whole)
    dots = jnp.concatenate(dots, axis=1)
    row_dot[...] = jnp.broadcast_to(dots, (8, 384))
    bands = [jnp.full((1, 384), band[0, i], jnp.int32).astype(F32) for i in range(2)]
    stack = [v.astype(F32) for v in parts_of(norm[:1]) + parts_of(dots)] + bands
    parcel[128:, :] = jnp.concatenate(stack, axis=0).astype(BF16)
    wait(copies)


def own_body(
    parcel, row_dot, prob, query, keys, values, grad_query, key_part, value_part
):
    for h in range(3):
        g = parcel[:128, lanes(h)]
        total = None
        for i in range(4):
            p = prob[h, 128 * i : 128 * i + 128]
            s = p * (dot(values[i, :, lanes(h)], g, 1, 1) - row_dot[:1, lanes(h)])
            s = s.astype(BF16)
            part = dot(s, keys[i, :, lanes(h)], 0, 0)
            total = part if total is None else total + part
            if i == 0:
                key_part[:, lanes(h)] = dot(s, query[:, lanes(h)], 1, 0)
                value_part[:, lanes(h)] = dot(p.astype(BF16), g, 1, 0)
        grad_query[:, lanes(h)] = (SCALE * total).astype(BF16)


def later_body(frame, a1, a2, a4, later, score, values, key_part, value_part, grad_key, grad_value):
    spread = jnp.abs(iota((128, 128), 0) - iota((128, 128), 1)).astype(F32)
    for h in range(3):
        keys, vals = key_part[:, lanes(h)], value_part[:, lanes(h)]
        for i, (d, box) in enumerate(((1, a1), (2, a2), (4, a4))):
            extra = box[128:, lanes(h)].astype(F32)
            norm = extra[0:1] + extra[1:2] + extra[2:3]
            row_dot = extra[3:4] + extra[4:5] + extra[5:6]
            limit = jnp.full((1, 128), 128.0, F32) if d == 1 else extra[5 + d // 2 : 6 + d // 2]
            limit = jnp.where(frame[0] + d < 128, limit, 0.0)
            p = jnp.where(spread < limit, jnp.exp(score[3 * i + h] - norm), 0.0)
            g = box[:128, lanes(h)]
            s = (p * (dot(values[0, :, lanes(h)], g, 1, 1) - row_dot)).astype(BF16)
            keys = keys + dot(s, later[i, :, lanes(h)], 1, 0)
            vals = vals + dot(p.astype(BF16), g, 1, 0)
        grad_key[:, lanes(h)] = (SCALE * keys).astype(BF16)
        grad_value[:, lanes(h)] = vals.astype(BF16)


def step(
    grad_out, out_weight, row_owner, row_position, query_rows, key_rows, value_rows, band_widths
):
    frame = lax.axis_index(SEQ).reshape(1)

    packed, pair = call(
        pack_body,
        [((16, 104, LANES), BF16), ((128, 768), BF16)],
        "s" + "h" * 6 + "vv",
        (frame, row_owner[None], row_position[None], grad_out, out_weight.T, key_rows, value_rows),
        13_000_000,
        [((1, 128), jnp.int32), ((1, 128), jnp.int32), ((128, 384), BF16), ((24, 384), BF16)],
        6,
    )
    got = exchange(packed, "z")
    pairs, later = [], []
    for d in DISTANCES[1:]:
        pairs.append(shifted(pair, d))
    for d in DISTANCES[1:]:
        later.append(shifted(query_rows, -d))
    own, rows = call(
        split_body, [((16, 80, LANES), BF16), ((8, 8, 48, LANES), BF16)], "vhv", (got,), 100_000_000, (), 1
    )
    rows = exchange(rows.reshape(64, 48, LANES), ("head", "x", "core")).reshape(8, 8, 48, LANES)

    right = turned(own, "x", 1)
    left = turned(own, "x", -1)
    far = turned(left, "x", -1)
    prob, norm, score = call(
        forward_body,
        [((3, 512, 128), F32), ((8, 384), F32), ((9, 128, 128), F32)],
        "ss" + "h" * 12,
        (frame, band_widths, query_rows, key_rows, value_rows, *pairs, *later),
        90_000_000,
        [((128, 384), BF16), ((128, 384), BF16), ((3, 128, 384), BF16), ((3, 128, 384), BF16)]
        + [((3, 512, 128), F32), ((8, 384), F32), ((9, 128, 128), F32)],
        8,
    )
    rows, far, left, prob, norm, score = lax.optimization_barrier((rows, far, left, prob, norm, score))

    mine, yours, keys, values, prob, norm = call(
        project_body,
        [((152, 384), F32)] * 2 + [((4, 128, 384), BF16)] * 2 + [((3, 512, 128), F32), ((8, 384), F32)],
        "svhv" + "h" * 9 + "v" * 6,
        (frame, rows, own, right, far, left, key_rows, value_rows, *pairs, prob, norm),
        350_000_000,
        [((16, 4, 24, 384), BF16), ((4, 16, 8, LANES), BF16)],
        26,
    )
    other = turned(yours, "core", 1)
    parcel, row_dot, query, later, score = call(
        finish_body,
        [((136, 384), BF16), ((8, 384), F32), ((128, 384), BF16), ((3, 128, 384), BF16), ((9, 128, 128), F32)],
        "ss" + "v" * 5 + "h" * 5 + "v" * 5,
        (frame, band_widths, mine, other, values, prob, norm, query_rows, *later, score),
        50_000_000,
        (),
        5,
    )
    boxes = []
    for d in DISTANCES[1:]:
        boxes.append(shifted(parcel, -d))
    grad_query, key_part, value_part = call(
        own_body,
        [((128, 384), BF16), ((128, 384), F32), ((128, 384), F32)],
        "v" * 9,
        (parcel, row_dot, prob, query, keys, values),
        120_000_000,
    )
    grad_key, grad_value = call(
        later_body,
        [((128, 384), BF16), ((128, 384), BF16)],
        "s" + "v" * 10,
        (frame, *boxes, later, score, values, key_part, value_part),
        120_000_000,
    )
    return grad_query, grad_key, grad_value


def solution(mesh):
    grid = mesh.devices.reshape(tuple(SIZES.values()) + (mesh.shape["head"],))
    fine = Mesh(grid, tuple(SIZES) + ("head",))
    return jax.shard_map(
        step,
        mesh=fine,
        in_specs=(
            P(SEQ, "head"),
            P("head", SEQ),
            P(SEQ),
            P(SEQ),
            P(SEQ, "head"),
            P(SEQ, "head"),
            P(SEQ, "head"),
            P(SEQ, None),
        ),
        out_specs=(P(SEQ, "head"), P(SEQ, "head"), P(SEQ, "head")),
        check_vma=False,
    )
```

```python
import functools

import jax
import jax.numpy as jnp
from jax import lax
from jax.experimental import pallas as pl
from jax.experimental.pallas import tpu as pltpu
from jax.sharding import Mesh
from jax.sharding import PartitionSpec as P


HEAD_DIM = 128
LANES = 128
DISTANCES = (0, 1, 2, 4)
NEG_FILL = -1e30
SEQ = ("z", "x", "core")
SIZES = {"z": 16, "x": 4, "core": 2}
F32 = jnp.float32
BF16 = jnp.bfloat16
SCALE = HEAD_DIM ** (-0.5)


def shifted(value, by):
    peers = lax.axis_size(SEQ)
    pairs = [(i, i + by) for i in range(peers) if 0 <= i + by < peers]
    return lax.ppermute(value, SEQ, pairs)


def turned(value, axis, by):
    peers = lax.axis_size(axis)
    return lax.ppermute(value, axis, [(i, (i + by) % peers) for i in range(peers)])


def exchange(value, axis):
    return lax.all_to_all(value, axis, split_axis=0, concat_axis=0, tiled=True)


def dot(a, b, left, right):
    return lax.dot_general(a, b, (((left,), (right,)), ((), ())), preferred_element_type=F32)


SPACES = {"s": pltpu.SMEM, "v": pltpu.VMEM, "h": pltpu.HBM}


def call(body, outs, spaces, args, flops, scratch=(), copies=0):
    specs = [pl.BlockSpec(memory_space=SPACES[c]) for c in spaces]
    size = sum(a.size * a.dtype.itemsize for a in args)
    size += sum(int(jnp.dtype(t).itemsize) * functools.reduce(lambda m, n: m * n, s) for s, t in outs)
    args = [pltpu.with_memory_space_constraint(a, pltpu.HBM) if c == "h" else a for a, c in zip(args, spaces)]
    scratch = [pltpu.VMEM(shape, kind) for shape, kind in scratch]
    if copies:
        scratch.append(pltpu.SemaphoreType.DMA((copies,)))
    return pl.pallas_call(
        body,
        out_shape=[
            pltpu.HBM(s, t) if c == "h" else jax.ShapeDtypeStruct(s, t)
            for (s, t), c in zip(outs, spaces[len(args) :])
        ],
        in_specs=specs[: len(args)],
        out_specs=specs[len(args) :],
        scratch_shapes=scratch,
        cost_estimate=pl.CostEstimate(flops=flops, bytes_accessed=size, transcendentals=0),
        compiler_params=pltpu.CompilerParams(vmem_limit_bytes=8 * 2**20),
    )(*args)


def started(pairs, sems):
    copies = [pltpu.make_async_copy(a, b, sems.at[i]) for i, (a, b) in enumerate(pairs)]
    for copy in copies:
        copy.start()
    return copies


def wait(copies):
    for copy in copies:
        copy.wait()


def iota(shape, dim):
    return lax.broadcasted_iota(jnp.int32, shape, dim)


def lanes(h):
    return slice(h * LANES, (h + 1) * LANES)


def pack_body(frame, owner_h, place_h, grad_h, weight_h, key_h, value_h, out, pair, owner, place, grad, weight, sems):
    moves = ((owner_h, owner), (place_h, place), (grad_h, grad), (weight_h, weight))
    moves += ((key_h, pair.at[:, :384]), (value_h, pair.at[:, 384:]))
    copies = started(moves, sems)
    wait(copies[:4])
    pick = iota((128, 128), 0) == owner[...]
    where = jnp.sum(jnp.where(pick, place[...].astype(F32), 0.0), axis=1, keepdims=True)
    where = jnp.broadcast_to(where, (128, LANES)).astype(BF16)
    rows = dot(pick.astype(BF16), grad[...], 1, 0).astype(BF16)
    for h in range(3):
        piece = weight[:, lanes(h)]
        for z in range(16):
            out[z, 24 * h : 24 * h + 24, :] = piece
            out[z, 80 + 8 * h : 88 + 8 * h, :] = rows[8 * z : 8 * z + 8, lanes(h)]
    for z in range(16):
        out[z, 72:80, :] = where[8 * z : 8 * z + 8]
    wait(copies[4:])


def split_body(got, weight, rows, sems):
    copies = started(((got.at[:, :80, :], weight),), sems)
    row, col = iota((128, 128), 0), iota((128, 128), 1)
    order = (col == (row & 15) * 8 + (row >> 4)).astype(BF16)
    blocks = [
        dot(order, got[:, 80 + 8 * b : 88 + 8 * b, :].reshape(128, LANES), 1, 0) for b in range(3)
    ]
    cell = iota((1, 768), 1)
    core = (cell >= 384).astype(jnp.int32)
    at = cell - 384 * core
    place = jnp.where(at < 192, at, jnp.where(at >= 320, at - 192, -1))
    source = jnp.where(place >= 0, place + ((place * 2731) >> 16) * 24 + core * 24, -1)
    move = (iota((384, 768), 0) == source).astype(BF16)
    moved = dot(jnp.concatenate(blocks, axis=1).astype(BF16), move, 1, 0)
    for x in range(4):
        first, second = moved[32 * x : 32 * x + 16], moved[32 * x + 16 : 32 * x + 32]
        for c in range(2):
            begin = 3 * c
            block = [first[:, lanes(begin)], second[:, lanes(begin)]]
            block.append(first[:, lanes(begin + 1)] + second[:, lanes(begin + 2)])
            block = jnp.concatenate(block, axis=0).astype(BF16)
            for y in range(8):
                rows[y, 2 * x + c] = block
    wait(copies)


def forward_body(
    frame, band, query_h, key_h, value_h, b1, b2, b4, l1, l2, l4, prob_h, norm_h, score_h,
    query, key, pairs, later, prob, norm, score, sems
):
    moves = [(query_h, query), (key_h, key)]
    moves += [(b.at[:, :384], pairs.at[i]) for i, b in enumerate((b1, b2, b4))]
    moves += [(b, later.at[i]) for i, b in enumerate((l1, l2, l4))]
    wait(started(moves, sems))
    spread = jnp.abs(iota((128, 128), 0) - iota((128, 128), 1))
    f = frame[0]
    limits = [
        None,
        jnp.where(f >= 1, 128, 0),
        jnp.where(f >= 2, band[0, 0], 0),
        jnp.where(f >= 4, band[0, 1], 0),
    ]
    for h in range(3):
        q = query[:, lanes(h)]
        parts = []
        for i, limit in enumerate(limits):
            keys = key[:, lanes(h)] if i == 0 else pairs[i - 1, :, lanes(h)]
            s = dot(keys, q, 1, 1) * SCALE
            parts.append(s if limit is None else jnp.where(spread < limit, s, NEG_FILL))
        s = jnp.concatenate(parts, axis=0)
        top = jnp.max(s, axis=0, keepdims=True)
        w = jnp.exp(s - top)
        total = jnp.sum(w, axis=0, keepdims=True)
        prob[h] = w / total
        norm[:, lanes(h)] = jnp.broadcast_to(top + jnp.log(total), (8, 128))
        for i in range(3):
            score[3 * i + h] = dot(key[:, lanes(h)], later[i, :, lanes(h)], 1, 1) * SCALE
    wait(started(((prob, prob_h), (norm, norm_h), (score, score_h)), sems))


def parts_of(value):
    high = value.astype(BF16)
    rest = value - high.astype(F32)
    middle = rest.astype(BF16)
    return high, middle, (rest - middle.astype(F32)).astype(BF16)


def project_body(
    frame, rows, o0, o1, o2, o3, key_h, value_h, b1, b2, b4, prob_h, norm_h, query_h, l1, l2, l4, score_h,
    mine, yours, keys, values, prob, norm, query, later, score, weight, places, sems
):
    x, core = (frame[0] >> 1) & 3, frame[0] & 1
    moves = []
    for turn, piece in enumerate((o0, o1, o2, o3)):
        to_x = (x + 4 - turn) & 3
        for h in range(3):
            moves.append((piece.at[:, 24 * h : 24 * h + 24, :], weight.at[:, to_x, :, lanes(h)]))
        moves.append((piece.at[:, 72:80, :], places.at[to_x]))
    moves += [(key_h, keys.at[0]), (value_h, values.at[0]), (prob_h, prob), (norm_h, norm)]
    for i, pair in enumerate((b1, b2, b4)):
        moves += [(pair.at[:, :384], keys.at[i + 1]), (pair.at[:, 384:], values.at[i + 1])]
    moves += [(query_h, query), (score_h, score)]
    moves += [(b, later.at[i]) for i, b in enumerate((l1, l2, l4))]
    copies = started(moves, sems)
    wait(copies[:16])
    low = (iota((128, 128), 1) < 64).astype(F32).astype(BF16)
    high = (iota((128, 128), 1) >= 64).astype(F32).astype(BF16)
    total = None
    for y in range(8):
        rest = rows[y, :, 32:48, :].reshape(128, LANES)
        both = [
            jnp.concatenate([rows[y, :, 16 * c : 16 * c + 16, :].reshape(128, LANES), rest * side], axis=1)
            for c, side in enumerate((low, high))
        ]
        block = weight[2 * y : 2 * y + 2].reshape(192, 384)
        block = jnp.concatenate([block, block[128:]], axis=0)
        part = dot(jnp.concatenate(both, axis=0), block, 1, 0)
        total = part if total is None else total + part
    where = places[...].astype(F32).reshape(64, 8, LANES)
    for out, frame_core, half in (
        (mine, core, jnp.where(core == 0, total[:128], total[128:])),
        (yours, 1 - core, jnp.where(core == 0, total[128:], total[:128])),
    ):
        out[:128, :] = half
        at = jnp.sum(jnp.where(iota((64, 8, LANES), 1) == 2 * x + frame_core, where, 0.0), axis=1)
        tail = jnp.concatenate([at[48:], jnp.zeros((8, LANES), F32)], axis=0)
        out[128:, :] = jnp.concatenate([at[:24], at[24:48], tail], axis=1)
    wait(copies[16:])


def places_of(half):
    return jnp.concatenate([half[128:, lanes(0)], half[128:, lanes(1)], half[128:144, lanes(2)]], axis=0)


def finish_body(frame, band, mine, other, values, prob, norm, parcel, row_dot):
    core = frame[0] & 1
    packed = (mine[:128, :] + other[:128, :]).astype(BF16)
    own, far = places_of(mine), places_of(other)
    first, second = jnp.where(core == 0, own, far), jnp.where(core == 0, far, own)
    where = []
    for x in range(4):
        where += [first[16 * x : 16 * x + 16], second[16 * x : 16 * x + 16]]
    where = jnp.concatenate(where, axis=0) == iota((128, 128), 1).astype(F32)
    grad = dot(where.astype(F32).astype(BF16), packed, 0, 0).astype(BF16)
    parcel[:128, :] = grad
    dots = []
    for h in range(3):
        g = grad[:, lanes(h)]
        whole = jnp.zeros((1, 128), F32)
        for i in range(4):
            p = prob[h, 128 * i : 128 * i + 128].astype(BF16).astype(F32)
            whole = whole + jnp.sum(p * dot(values[i, :, lanes(h)], g, 1, 1), axis=0, keepdims=True)
        dots.append(whole)
    dots = jnp.concatenate(dots, axis=1)
    row_dot[...] = jnp.broadcast_to(dots, (8, 384))
    bands = [jnp.full((1, 384), band[0, i], jnp.int32).astype(F32) for i in range(2)]
    stack = [v.astype(F32) for v in parts_of(norm[:1]) + parts_of(dots)] + bands
    parcel[128:, :] = jnp.concatenate(stack, axis=0).astype(BF16)


def own_body(
    parcel, row_dot, prob, query, keys, values, grad_query, key_part, value_part
):
    for h in range(3):
        g = parcel[:128, lanes(h)]
        total = None
        for i in range(4):
            p = prob[h, 128 * i : 128 * i + 128]
            s = p * (dot(values[i, :, lanes(h)], g, 1, 1) - row_dot[:1, lanes(h)])
            s = s.astype(BF16)
            part = dot(s, keys[i, :, lanes(h)], 0, 0)
            total = part if total is None else total + part
            if i == 0:
                key_part[:, lanes(h)] = dot(s, query[:, lanes(h)], 1, 0)
                value_part[:, lanes(h)] = dot(p.astype(BF16), g, 1, 0)
        grad_query[:, lanes(h)] = (SCALE * total).astype(BF16)


def later_body(frame, a1, a2, a4, later, score, values, key_part, value_part, grad_key, grad_value):
    spread = jnp.abs(iota((128, 128), 0) - iota((128, 128), 1)).astype(F32)
    for h in range(3):
        keys, vals = key_part[:, lanes(h)], value_part[:, lanes(h)]
        for i, (d, box) in enumerate(((1, a1), (2, a2), (4, a4))):
            extra = box[128:, lanes(h)].astype(F32)
            norm = extra[0:1] + extra[1:2] + extra[2:3]
            row_dot = extra[3:4] + extra[4:5] + extra[5:6]
            limit = jnp.full((1, 128), 128.0, F32) if d == 1 else extra[5 + d // 2 : 6 + d // 2]
            limit = jnp.where(frame[0] + d < 128, limit, 0.0)
            p = jnp.where(spread < limit, jnp.exp(score[3 * i + h] - norm), 0.0)
            g = box[:128, lanes(h)]
            s = (p * (dot(values[0, :, lanes(h)], g, 1, 1) - row_dot)).astype(BF16)
            keys = keys + dot(s, later[i, :, lanes(h)], 1, 0)
            vals = vals + dot(p.astype(BF16), g, 1, 0)
        grad_key[:, lanes(h)] = (SCALE * keys).astype(BF16)
        grad_value[:, lanes(h)] = vals.astype(BF16)


def step(
    grad_out, out_weight, row_owner, row_position, query_rows, key_rows, value_rows, band_widths
):
    frame = lax.axis_index(SEQ).reshape(1)

    packed, pair = call(
        pack_body,
        [((16, 104, LANES), BF16), ((128, 768), BF16)],
        "s" + "h" * 6 + "vv",
        (frame, row_owner[None], row_position[None], grad_out, out_weight.T, key_rows, value_rows),
        13_000_000,
        [((1, 128), jnp.int32), ((1, 128), jnp.int32), ((128, 384), BF16), ((24, 384), BF16)],
        6,
    )
    got = exchange(packed, "z")
    pairs, later = [], []
    for d in DISTANCES[1:]:
        pairs.append(shifted(pair, d))
    for d in DISTANCES[1:]:
        later.append(shifted(query_rows, -d))
    own, rows = call(
        split_body, [((16, 80, LANES), BF16), ((8, 8, 48, LANES), BF16)], "vhv", (got,), 100_000_000, (), 1
    )
    rows = exchange(rows.reshape(64, 48, LANES), ("head", "x", "core")).reshape(8, 8, 48, LANES)

    right = turned(own, "x", 1)
    left = turned(own, "x", -1)
    far = turned(left, "x", -1)
    prob, norm, score = call(
        forward_body,
        [((3, 512, 128), F32), ((8, 384), F32), ((9, 128, 128), F32)],
        "ss" + "h" * 12,
        (frame, band_widths, query_rows, key_rows, value_rows, *pairs, *later),
        90_000_000,
        [((128, 384), BF16), ((128, 384), BF16), ((3, 128, 384), BF16), ((3, 128, 384), BF16)]
        + [((3, 512, 128), F32), ((8, 384), F32), ((9, 128, 128), F32)],
        8,
    )
    rows, far, left, prob, norm, score = lax.optimization_barrier((rows, far, left, prob, norm, score))

    mine, yours, keys, values, prob, norm, query, later, score = call(
        project_body,
        [((152, 384), F32)] * 2
        + [((4, 128, 384), BF16)] * 2
        + [((3, 512, 128), F32), ((8, 384), F32), ((128, 384), BF16), ((3, 128, 384), BF16), ((9, 128, 128), F32)],
        "svhv" + "h" * 14 + "v" * 9,
        (frame, rows, own, right, far, left, key_rows, value_rows, *pairs, prob, norm, query_rows, *later, score),
        350_000_000,
        [((16, 4, 24, 384), BF16), ((4, 16, 8, LANES), BF16)],
        31,
    )
    other = turned(yours, "core", 1)
    parcel, row_dot = call(
        finish_body,
        [((136, 384), BF16), ((8, 384), F32)],
        "ss" + "v" * 7,
        (frame, band_widths, mine, other, values, prob, norm),
        50_000_000,
    )
    boxes = []
    for d in DISTANCES[1:]:
        boxes.append(shifted(parcel, -d))
    grad_query, key_part, value_part = call(
        own_body,
        [((128, 384), BF16), ((128, 384), F32), ((128, 384), F32)],
        "v" * 9,
        (parcel, row_dot, prob, query, keys, values),
        120_000_000,
    )
    grad_key, grad_value = call(
        later_body,
        [((128, 384), BF16), ((128, 384), BF16)],
        "s" + "v" * 10,
        (frame, *boxes, later, score, values, key_part, value_part),
        120_000_000,
    )
    return grad_query, grad_key, grad_value


def solution(mesh):
    grid = mesh.devices.reshape(tuple(SIZES.values()) + (mesh.shape["head"],))
    fine = Mesh(grid, tuple(SIZES) + ("head",))
    return jax.shard_map(
        step,
        mesh=fine,
        in_specs=(
            P(SEQ, "head"),
            P("head", SEQ),
            P(SEQ),
            P(SEQ),
            P(SEQ, "head"),
            P(SEQ, "head"),
            P(SEQ, "head"),
            P(SEQ, None),
        ),
        out_specs=(P(SEQ, "head"), P(SEQ, "head"), P(SEQ, "head")),
        check_vma=False,
    )
```
